256 devices in a mesh: row: 8 (over x, core), col: 32 (over y, z).
Axes of the slice: x: 4, y: 4, z: 8, core: 2. Of those that a mesh axis runs over, the one named last changes fastest.
Arguments:
- connectivity: int32 [4, 2097152], P(None, ('row', 'col')), may hold values from 0 to 3071
- gradients: float32 [9, 2097152], P(None, ('row', 'col')), may hold values from -4 to 4
- volumes: float32 [2097152], P(('row', 'col')), may hold values from 0.2 to 1
- live_blocks: int32 [256], P(('row', 'col')), may hold values from 1 to 8, as said below
- send_lists: int32 [4, 65536], P(None, ('row', 'col')), may hold values from 0 to 2047
- divergence: float32 [524288], P(('row', 'col')), may hold values from -6 to 6
- mass_shift: float32 [524288], P(('row', 'col')), may hold values from 0.5 to 4
- boundary_nodes: int32 [81920], P(('row', 'col')), may hold values from 0 to 2047
- surface_points: float32 [3, 81920], P(None, ('row', 'col')), may hold values from 0 to 1
- normal_cos: float32 [81920], P(('row', 'col')), may hold values from -1 to 1
- normal_angle: float32 [81920], P(('row', 'col')), may hold values from -3.140625 to 3.140625
- node_areas: float32 [81920], P(('row', 'col')), may hold values from 0.00036621094 to 0.0014648438
Outputs:
- potential: float32 [524288], P(('row', 'col'))
- dirichlet: float32 [8192], P(('row', 'col'))
The draws below stay inside these ranges and needn't reach their ends.
Inputs may be any that keep to these rules, and one draw needn't show every extreme that they name: The first live_blocks[p] element blocks of partition p are live, the rest are padding; some partition has all 8 blocks live. `connectivity`: indices into the partition's extended node list. `send_lists`: indices of the partition's own nodes. `boundary_nodes`: indices of the partition's own nodes.
All inputs are finite; a program needn't handle non-finite values.
Results may differ from the reference program's by a relative error of at most 0.0024.
Values sent between devices are 32-bit elements; how exact they have to be, the bound alone decides.
No kernel may reach another device: no remote copies, remote signals or barrier semaphores. Data moves between devices by JAX's collectives and lax.ppermute only.
A program may use at most 64 MiB of HBM per device.

```python
import math
import jax
import jax.numpy as jnp
from jax import lax

NN_DEV = 2048
TGT_DEV = 32
NBLK = 8
ITERS = 3
NB = 81920
NE_DEV = 8192
EBLK = 1024
GH = 256
NN = 524288
NE = 2097152
NT = 8192
N_ROW = 8
N_COL = 32


def draw_live_blocks(key, part):
    first, second, third = jax.random.split(key, 3)
    devices_total = N_ROW * N_COL
    left = jax.random.randint(first, (devices_total,), 0, 8)
    right = jax.random.randint(second, (devices_total,), 0, 8)
    counts = jnp.minimum(1 + left * right // 8, NBLK)
    fullest = jax.random.randint(third, (), 0, devices_total)
    return jnp.where(jnp.arange(devices_total) == fullest, NBLK, counts).astype(jnp.int32)


def set_ends(values, key, smallest, high):
    spot = [jax.random.randint(jax.random.fold_in(key, axis), (), 0, length) for axis, length in enumerate(values.shape)]
    widest = values.shape.index(max(values.shape))
    neighbour = spot[:widest] + [(spot[widest] + 1) % values.shape[widest]] + spot[widest + 1:]
    return values.at[tuple(spot)].set(smallest).at[tuple(neighbour)].set(high)


def levels(stream_key, dims, cuts, low, top_value):
    factor_of, own = 1.0, jax.random.fold_in(stream_key, 6)
    for dim, parts in cuts:
        steps = jnp.exp(jax.random.uniform(jax.random.fold_in(own, dim), (parts,), jnp.float32, low / len(cuts), top_value / len(cuts)))
        factor_of = factor_of * jnp.repeat(steps, dims[dim] // parts).reshape([-1 if axis == dim else 1 for axis in range(len(dims))])
    return factor_of


def normal_values(own_key, dims, spread, most, cuts=(), kind=jnp.bfloat16):
    result = spread * jax.random.normal(own_key, dims, jnp.float32)
    if cuts:
        result = result * levels(own_key, dims, cuts, -0.22, 0.18)
    return jnp.clip(result, -most, most).astype(kind)


def setup_inputs(seed: int = 0) -> dict:
    arg_keys = jax.random.split(jax.random.key(seed), 13)
    return {
        "connectivity": set_ends(jax.random.randint(arg_keys[0], (4, NE), 0, NN_DEV + 4 * GH), jax.random.fold_in(arg_keys[0], 1), 0, (NN_DEV + 4 * GH) - 1).astype(jnp.int32),
        "gradients": normal_values(arg_keys[1], (9, NE), 0.5, 4.0, ((1, 256),), jnp.float32),
        "volumes": jnp.clip(jnp.exp(math.log(1.0) - 1.609438 * jax.random.uniform(arg_keys[2], (NE,), jnp.float32) ** levels(arg_keys[2], (NE,), ((0, 256),), -0.2, 0.2)), 0.2, 1.0),
        "live_blocks": draw_live_blocks(jax.random.fold_in(arg_keys[12], 71), 0),
        "send_lists": set_ends(jax.random.randint(arg_keys[4], (4, GH * N_ROW * N_COL), 0, NN_DEV), jax.random.fold_in(arg_keys[4], 1), 0, NN_DEV - 1).astype(jnp.int32),
        "divergence": normal_values(arg_keys[5], (NN,), 1.0, 6.0, ((0, 256),), jnp.float32),
        "mass_shift": jnp.clip(jnp.exp(math.log(4.0) - 2.0794415 * jax.random.uniform(arg_keys[6], (NN,), jnp.float32) ** levels(arg_keys[6], (NN,), ((0, 256),), -0.2, 0.2)), 0.5, 4.0),
        "boundary_nodes": set_ends(jax.random.randint(arg_keys[7], (NB,), 0, NN_DEV), jax.random.fold_in(arg_keys[7], 1), 0, NN_DEV - 1).astype(jnp.int32),
        "surface_points": jnp.clip(1.0 * jax.random.uniform(arg_keys[8], (3, NB), jnp.float32) ** levels(arg_keys[8], (3, NB), ((1, 256),), -0.2, 0.2), 0.0, 1.0),
        "normal_cos": jnp.clip(jax.random.uniform(arg_keys[9], (NB,), jnp.float32, -1.0, 1.0) * levels(arg_keys[9], (NB,), ((0, 256),), -0.4, 0.0), -1.0, 1.0),
        "normal_angle": jnp.clip(jax.random.uniform(arg_keys[10], (NB,), jnp.float32, -3.140625, 3.140625), -3.140625, 3.140625),
        "node_areas": jnp.clip(jnp.exp(math.log(0.0014648438) - 1.3862944 * jax.random.uniform(arg_keys[11], (NB,), jnp.float32) ** levels(arg_keys[11], (NB,), ((0, 256),), -0.2, 0.2)), 0.00036621094, 0.0014648438),
    }


smoothing = 0.0001
inverse_four_pi = 1.0 / (4.0 * math.pi)

def pick_block(total, largest):
    for candidate in range(min(total, largest), 0, -1):
        if total % candidate == 0:
            return candidate
    return 1

def element_apply(extended, corners, gradients, volumes):
    corner_values = extended[corners]
    grad_zero = gradients[0:3]
    grad_one = gradients[3:6]
    grad_two = gradients[6:9]
    grad_three = -(grad_zero + grad_one + grad_two)
    field_grad = grad_zero * corner_values[0] + grad_one * corner_values[1] + grad_two * corner_values[2] + grad_three * corner_values[3]
    corner_terms = jnp.stack([lax.optimization_barrier(jnp.sum(gradient * field_grad, axis=0)) for gradient in (grad_zero, grad_one, grad_two, grad_three)]) * volumes
    return jnp.zeros(extended.shape, jnp.float32).at[corners].add(corner_terms)

def kernel_rows(targets, sources):
    delta_x = targets[0][:, None] - sources[0][None, :]
    delta_y = targets[1][:, None] - sources[1][None, :]
    delta_z = targets[2][:, None] - sources[2][None, :]
    radius_sq = delta_x * delta_x + delta_y * delta_y + delta_z * delta_z + smoothing
    inverse = lax.rsqrt(radius_sq)
    numerator = delta_x * sources[3][None, :] + delta_y * sources[4][None, :] + delta_z * sources[5][None, :]
    entries = (numerator * (inverse * inverse * inverse) * inverse_four_pi).astype(jnp.bfloat16)
    return jnp.dot(entries, sources[6].astype(jnp.bfloat16), preferred_element_type=jnp.float32)

def reference(connectivity, gradients, volumes, live_blocks, send_lists, divergence, mass_shift, boundary_nodes, surface_points, normal_cos, normal_angle, node_areas):
    rows = N_ROW
    cols = N_COL
    corners = connectivity.reshape(4, rows, cols, NE_DEV).transpose(1, 2, 0, 3)
    grads = gradients.reshape(9, rows, cols, NE_DEV).transpose(1, 2, 0, 3)
    lists = send_lists.reshape(4, rows, cols, GH).transpose(1, 2, 0, 3)
    live = live_blocks.reshape(rows, cols)
    block_of = jnp.arange(NE_DEV, dtype=jnp.int32) // EBLK
    live_mask = (block_of[None, None, :] < live[:, :, None]).astype(jnp.float32)
    masked_volumes = volumes.reshape(rows, cols, NE_DEV) * live_mask
    shift_grid = mass_shift.reshape(rows, cols, NN_DEV)
    zero_row = jnp.zeros((1, cols, GH), jnp.float32)
    zero_col = jnp.zeros((rows, 1, GH), jnp.float32)

    def operate(values):
        picked = jax.vmap(jax.vmap(lambda field, index: field[index]))(values, lists)
        from_lower_row = jnp.concatenate([zero_row, picked[:-1, :, 0]], axis=0)
        from_upper_row = jnp.concatenate([picked[1:, :, 1], zero_row], axis=0)
        from_lower_col = jnp.concatenate([zero_col, picked[:, :-1, 2]], axis=1)
        from_upper_col = jnp.concatenate([picked[:, 1:, 3], zero_col], axis=1)
        ghosts = jnp.stack([from_lower_row, from_upper_row, from_lower_col, from_upper_col], axis=2).reshape(rows, cols, 4 * GH)
        extended = jnp.concatenate([values, ghosts], axis=2)
        assembled = jax.vmap(jax.vmap(element_apply))(extended, corners, grads, masked_volumes)
        owned = assembled[:, :, :NN_DEV]
        ghost_terms = assembled[:, :, NN_DEV:].reshape(rows, cols, 4, GH)
        back_zero = jnp.concatenate([ghost_terms[1:, :, 0], zero_row], axis=0)
        back_one = jnp.concatenate([zero_row, ghost_terms[:-1, :, 1]], axis=0)
        back_two = jnp.concatenate([ghost_terms[:, 1:, 2], zero_col], axis=1)
        back_three = jnp.concatenate([zero_col, ghost_terms[:, :-1, 3]], axis=1)
        returned = jnp.stack([back_zero, back_one, back_two, back_three], axis=2)
        owned = jax.vmap(jax.vmap(lambda field, index, terms: field.at[index].add(terms)))(owned, lists, returned)
        return shift_grid * values + owned
    residual = divergence.reshape(rows, cols, NN_DEV)
    direction = residual
    potential = jnp.zeros_like(residual)
    norm_now = jnp.sum(residual * residual)
    for iteration in range(ITERS):
        image = operate(direction)
        alpha = norm_now / jnp.sum(direction * image)
        potential = potential + alpha * direction
        residual = residual - alpha * image
        norm_next = jnp.sum(residual * residual)
        direction = residual + norm_next / norm_now * direction
        norm_now = norm_next
    slots = NB // (rows * cols)
    traces = jnp.take_along_axis(potential.reshape(rows * cols, NN_DEV), boundary_nodes.reshape(rows * cols, slots), axis=1)
    trace_bf = traces.reshape(NB).astype(jnp.bfloat16)
    sine = jnp.sqrt(1.0 - normal_cos * normal_cos)
    normals = jnp.stack([sine * jnp.cos(normal_angle), sine * jnp.sin(normal_angle), normal_cos])
    weighted = node_areas[None, :] * normals
    sources = jnp.concatenate([surface_points, weighted, trace_bf.astype(jnp.float32)[None, :]], axis=0)
    target_points = surface_points.reshape(3, rows * cols, slots)[:, :, :TGT_DEV].reshape(3, NT)
    target_traces = traces[:, :TGT_DEV].reshape(NT)
    step = pick_block(NT, 512)
    target_blocks = target_points.reshape(3, NT // step, step).transpose(1, 0, 2)
    far_field = lax.map(lambda targets: kernel_rows(targets, sources), target_blocks).reshape(NT)
    dirichlet = far_field - 0.5 * target_traces
    return (potential.reshape(NN), dirichlet)
```

```python
import functools
import math

import jax
import jax.numpy as jnp
from jax import lax
from jax.experimental import pallas as pl
from jax.experimental.pallas import tpu as pltpu
from jax.sharding import PartitionSpec as P

F32 = jnp.float32
BF16 = jnp.bfloat16
LANES = 128
NN_DEV = 2048
NE_DEV = 8192
EBLK = 1024
GH = 256
TGT_DEV = 32
OWN_ROWS = NN_DEV // LANES
GHOST_ROWS = 4 * GH // LANES
EXT_ROWS = OWN_ROWS + GHOST_ROWS
ELEM_ROWS = NE_DEV // LANES
SLOTS = 320
PAD_SLOTS = 384
N_DEV = 256
SPLITS = 3
SCALE = 1.0 / 64.0
smoothing = 0.0001
inverse_four_pi = 1.0 / (4.0 * math.pi)


def gather_rows(table, index):
    rows = table.shape[0]
    high = index >> 7
    low = index & 127
    out = jnp.zeros(index.shape, F32)
    for r in range(rows):
        row = jnp.broadcast_to(table[r:r + 1, :], index.shape)
        out = jnp.where(high == r, jnp.take_along_axis(row, low, axis=1), out)
    return out


def split_terms(terms):
    parts = []
    rest = terms
    for _ in range(SPLITS):
        part = rest.astype(BF16)
        parts.append(part.astype(F32))
        rest = rest - parts[-1]
    return parts


def scatter_block(index_rows, term_rows, rows):
    sub = lax.broadcasted_iota(jnp.int32, (LANES, LANES), 0)
    sub_rows = lax.broadcasted_iota(jnp.int32, (rows, LANES), 0)
    hot_blocks = []
    weight_blocks = []
    for index, terms in zip(index_rows, term_rows):
        low = jnp.broadcast_to(index & 127, (LANES, LANES))
        hot_blocks.append(jnp.where(sub == low, 1.0, 0.0).astype(BF16))
        mine = sub_rows == jnp.broadcast_to(index >> 7, (rows, LANES))
        pieces = [
            jnp.where(mine, jnp.broadcast_to(part, (rows, LANES)), 0.0)
            for part in split_terms(terms)
        ]
        weight_blocks.append(jnp.concatenate(pieces, axis=0).astype(BF16))
    hot = jnp.concatenate(hot_blocks, axis=1)
    weights = jnp.concatenate(weight_blocks, axis=1)
    total = lax.dot_general(
        weights, hot, (((1,), (1,)), ((), ())), preferred_element_type=F32
    )
    out = total[0:rows]
    for k in range(1, SPLITS):
        out = out + total[k * rows:(k + 1) * rows]
    return out


def element_gradient(ext, conn_ref, grad_ref, t):
    block = pl.ds(pl.multiple_of(t * 8, 8), 8)
    corner = [gather_rows(ext, conn_ref[a, block, :]) for a in range(4)]
    grads = [grad_ref[c, block, :] for c in range(9)]
    base = corner[3]
    diff = [corner[a] - base for a in range(3)]
    field = [
        grads[k] * diff[0] + grads[3 + k] * diff[1] + grads[6 + k] * diff[2]
        for k in range(3)
    ]
    return grads, field


def live_volume(live_ref, vol_ref, t):
    block = pl.ds(pl.multiple_of(t * 8, 8), 8)
    return jnp.where(t < live_ref[0], vol_ref[block, :], 0.0)


def extend(parity_ref, v, ghosts):
    first = parity_ref[0] == 0
    second = parity_ref[1] == 0
    row_a, row_b, col_a, col_b = ghosts
    return jnp.concatenate(
        [
            v,
            jnp.where(first, row_b, row_a),
            jnp.where(first, row_a, row_b),
            jnp.where(second, col_b, col_a),
            jnp.where(second, col_a, col_b),
        ],
        axis=0,
    )


def put_outgoing(parity_ref, blocks, out_refs):
    first = parity_ref[0] == 0
    second = parity_ref[1] == 0
    out_refs[0][...] = jnp.where(first, blocks[0], blocks[1])
    out_refs[1][...] = jnp.where(first, blocks[1], blocks[0])
    out_refs[2][...] = jnp.where(second, blocks[2], blocks[3])
    out_refs[3][...] = jnp.where(second, blocks[3], blocks[2])


def blocks_of(rows):
    return [rows[2 * d:2 * d + 2] for d in range(4)]


def pick_kernel(parity_ref, v_ref, list_ref, *out_refs):
    put_outgoing(parity_ref, blocks_of(gather_rows(v_ref[...], list_ref[...])), out_refs)


def apply_kernel(parity_ref, live_ref, v_ref, ga, gb, gc, gd, conn_ref, grad_ref, vol_ref,
                 own_ref, oa, ob, oc, od, ext_ref, term_ref, acc_ref):
    ext_ref[...] = extend(parity_ref, v_ref[...], [ga[...], gb[...], gc[...], gd[...]])

    def element_block(t, carry):
        ext = ext_ref[...]
        grads, field = element_gradient(ext, conn_ref, grad_ref, t)
        vol = live_volume(live_ref, vol_ref, t)
        block = pl.ds(pl.multiple_of(t * 8, 8), 8)
        field = [vol * f for f in field]
        last = jnp.zeros_like(vol)
        for a in range(3):
            term = grads[3 * a] * field[0] + grads[3 * a + 1] * field[1] + grads[3 * a + 2] * field[2]
            term_ref[a, block, :] = term
            last = last - term
        term_ref[3, block, :] = last
        return carry

    lax.fori_loop(0, NE_DEV // EBLK, element_block, 0)
    acc_ref[...] = jnp.zeros_like(acc_ref)

    def scatter_step(t, carry):
        block = pl.ds(pl.multiple_of(t * 8, 8), 8)
        total = acc_ref[...]
        for a in range(4):
            index = conn_ref[a, block, :]
            terms = term_ref[a, block, :]
            total = total + scatter_block(
                [index[s:s + 1] for s in range(8)], [terms[s:s + 1] for s in range(8)], EXT_ROWS
            )
        acc_ref[...] = total
        return carry

    lax.fori_loop(0, NE_DEV // EBLK, scatter_step, 0)
    own_ref[...] = acc_ref[0:OWN_ROWS, :]
    put_outgoing(parity_ref, swap_pairs(blocks_of(acc_ref[OWN_ROWS:EXT_ROWS, :])), (oa, ob, oc, od))


def swap_pairs(blocks):
    return [blocks[1], blocks[0], blocks[3], blocks[2]]


def combine_kernel(parity_ref, own_ref, ra, rb, rc, rd, list_ref, v_ref, mass_ref,
                   next_ref, oa, ob, oc, od):
    first = parity_ref[0] == 0
    second = parity_ref[1] == 0
    lists = list_ref[...]
    returned = jnp.concatenate(
        [
            jnp.where(first, ra[...], rb[...]),
            jnp.where(first, rb[...], ra[...]),
            jnp.where(second, rc[...], rd[...]),
            jnp.where(second, rd[...], rc[...]),
        ],
        axis=0,
    )
    added = scatter_block(
        [lists[s:s + 1] for s in range(8)], [returned[s:s + 1] for s in range(8)], OWN_ROWS
    )
    value = (mass_ref[...] * v_ref[...] + own_ref[...] + added) * SCALE
    next_ref[...] = value
    put_outgoing(parity_ref, blocks_of(gather_rows(value, lists)), (oa, ob, oc, od))


def far_kernel(parity_ref, live_ref, b_ref, v1_ref, v2_ref, ga, gb, gc, gd, conn_ref, grad_ref, vol_ref,
               mass_ref, node_ref, src_ref, tgt_ref,
               out_ref, trace_ref, ext_ref, tx, ty, tz, d0, d1, d2, lhs_ref):
    b = b_ref[...]
    v1 = v1_ref[...]
    v2 = v2_ref[...]
    ext_ref[...] = extend(parity_ref, v2, [ga[...], gb[...], gc[...], gd[...]])

    def energy_block(t, total):
        ext = ext_ref[...]
        _, field = element_gradient(ext, conn_ref, grad_ref, t)
        vol = live_volume(live_ref, vol_ref, t)
        return total + vol * (field[0] * field[0] + field[1] * field[1] + field[2] * field[2])

    energy = lax.fori_loop(0, NE_DEV // EBLK, energy_block, jnp.zeros((8, LANES), F32))
    pairs = [b * b, b * v1, v1 * v1, v1 * v2, v2 * v2, mass_ref[...] * v2 * v2]
    sums = [p[0:8] + p[8:16] for p in pairs]
    sums[5] = (sums[5] + energy) * SCALE
    sub = lax.broadcasted_iota(jnp.int32, (8, LANES), 0)
    lane_row = lax.broadcasted_iota(jnp.int32, (1, LANES), 1)
    moments = jnp.zeros((1, LANES), F32)
    for k in range(6):
        moments = jnp.where(lane_row == 96 + k, jnp.sum(sums[k]), moments)

    nodes = node_ref[...]
    traces = [gather_rows(table, nodes) for table in (b, v1, v2)]
    for k in range(3):
        trace_ref[k] = traces[k]
    slot = lax.broadcasted_iota(jnp.int32, (8, LANES), 0) * LANES + lax.broadcasted_iota(jnp.int32, (8, LANES), 1)
    for r in range(PAD_SLOTS // LANES):
        block = jnp.zeros((8, LANES), F32)
        for k in range(3):
            t = jnp.where(slot < SLOTS, traces[k], 0.0)[r:r + 1, :]
            high = t.astype(BF16).astype(F32)
            block = jnp.where(sub == 2 * k, high, block)
            block = jnp.where(sub == 2 * k + 1, t - high, block)
        lhs_ref[:, r * LANES:(r + 1) * LANES] = block.astype(BF16)

    lane = lax.broadcasted_iota(jnp.int32, (N_DEV // 4, LANES), 1)
    for c, ref in enumerate((tx, ty, tz)):
        out = jnp.zeros((N_DEV // 4, LANES), F32)
        for j in range(4):
            part = tgt_ref[pl.ds(j, N_DEV // 4, stride=4), :]
            shift = (32 * j - 32 * c) % LANES
            if shift:
                part = pltpu.roll(part, shift, 1)
            out = jnp.where((lane >= 32 * j) & (lane < 32 * j + 32), part, out)
        ref[...] = out

    cols = jnp.transpose(src_ref[...])

    def target_row(g, carry):
        at = pl.ds(g, 1)
        px = tx[at, :]
        py = ty[at, :]
        pz = tz[at, :]
        dx = px - cols[:, 0:1]
        dy = py - cols[:, 1:2]
        dz = pz - cols[:, 2:3]
        radius_sq = dx * dx + dy * dy + dz * dz + smoothing
        inverse = lax.rsqrt(radius_sq)
        numerator = dx * cols[:, 3:4] + dy * cols[:, 4:5] + dz * cols[:, 5:6]
        entries = (numerator * (inverse * inverse * inverse)).astype(BF16)
        res = jnp.dot(lhs_ref[...], entries, preferred_element_type=F32)
        d0[at, :] = res[0:1] + res[1:2]
        d1[at, :] = res[2:3] + res[3:4]
        d2[at, :] = res[4:5] + res[5:6]
        return carry

    lax.fori_loop(0, N_DEV // 4, target_row, 0)
    spread = jnp.broadcast_to(moments, (N_DEV // 4, LANES))
    for j in range(4):
        out = spread
        for k, ref in enumerate((d0, d1, d2)):
            part = ref[...]
            shift = (32 * k - 32 * j) % LANES
            if shift:
                part = pltpu.roll(part, shift, 1)
            out = jnp.where((lane >= 32 * k) & (lane < 32 * k + 32), part, out)
        out_ref[pl.ds(j, N_DEV // 4, stride=4), :] = out


def final_kernel(got_ref, b_ref, v1_ref, v2_ref, trace_ref, pot_ref, dir_ref):
    total = jnp.sum(got_ref[...], axis=0, keepdims=True)
    lane = lax.broadcasted_iota(jnp.int32, (1, LANES), 1)
    m = [jnp.sum(jnp.where(lane == 96 + k, total, 0.0), axis=1, keepdims=True) for k in range(6)]
    l1 = m[2] / m[1]
    l2 = m[3] / m[1]
    s11 = m[3] - l1 * m[2]
    s12 = m[4] - l1 * m[3]
    s22 = m[5] - l2 * m[3]
    y1 = m[1] - l1 * m[0]
    y2 = m[2] - l2 * m[0]
    keep1 = s11 > 4e-7 * m[3]
    safe11 = jnp.where(keep1, s11, 1.0)
    ratio = jnp.where(keep1, s12 / safe11, 0.0)
    d2 = s22 - ratio * s12
    keep2 = keep1 & (d2 > 4e-7 * m[5])
    c2 = jnp.where(keep2, (y2 - ratio * y1) / jnp.where(keep2, d2, 1.0), 0.0)
    c1 = jnp.where(keep1, (y1 - s12 * c2) / safe11, 0.0)
    c0 = (m[0] - m[2] * c1 - m[3] * c2) / m[1]
    c0 = c0 * SCALE
    c1 = c1 * SCALE
    c2 = c2 * SCALE
    pot_ref[...] = c0 * b_ref[...] + c1 * v1_ref[...] + c2 * v2_ref[...]
    out = jnp.zeros((1, LANES), F32)
    for k, c in enumerate((c0, c1, c2)):
        part = total
        if k:
            part = pltpu.roll(total, LANES - 32 * k, 1)
        out = out + c * (part - 0.5 * trace_ref[k, 0:1, :])
    dir_ref[...] = out


def call(body, out_shapes, smem, args, scratch=(), flops=1000000):
    specs = [pl.BlockSpec(memory_space=pltpu.SMEM)] * smem
    specs += [pl.BlockSpec(memory_space=pltpu.VMEM)] * (len(args) - smem)
    return pl.pallas_call(
        body,
        out_shape=[jax.ShapeDtypeStruct(s, F32) for s in out_shapes],
        in_specs=specs,
        out_specs=[pl.BlockSpec(memory_space=pltpu.VMEM)] * len(out_shapes),
        scratch_shapes=list(scratch),
    )(*args)


PIECE = (2, LANES)


def pairs(count, start):
    out = []
    for i in range(start, count - 1, 2):
        out += [(i, i + 1), (i + 1, i)]
    return out


def exchange(pieces):
    rows = lax.axis_size("row")
    cols = lax.axis_size("col")
    return [
        lax.ppermute(pieces[0], "row", pairs(rows, 0)),
        lax.ppermute(pieces[1], "row", pairs(rows, 1)),
        lax.ppermute(pieces[2], "col", pairs(cols, 0)),
        lax.ppermute(pieces[3], "col", pairs(cols, 1)),
    ]


def per_device(connectivity, gradients, volumes, live_blocks, send_lists, divergence, mass_shift,
               boundary_nodes, surface_points, normal_cos, normal_angle, node_areas):
    parity = jnp.stack([lax.axis_index("row") % 2, lax.axis_index("col") % 2]).astype(jnp.int32)
    conn = connectivity.reshape(4, ELEM_ROWS, LANES)
    grads = gradients.reshape(9, ELEM_ROWS, LANES)
    vol = volumes.reshape(ELEM_ROWS, LANES)
    lists = send_lists.reshape(4 * GH // LANES, LANES)
    b = divergence.reshape(OWN_ROWS, LANES)
    mass = mass_shift.reshape(OWN_ROWS, LANES)
    nodes = jnp.pad(boundary_nodes, (0, 8 * LANES - SLOTS)).reshape(8, LANES)

    own_targets = jnp.pad(surface_points[:, :TGT_DEV].reshape(1, 3 * TGT_DEV), ((0, 0), (0, TGT_DEV)))
    targets = lax.all_to_all(
        jnp.broadcast_to(own_targets, (N_DEV, LANES)), ("row", "col"), 0, 0, tiled=True
    )
    sine = jnp.sqrt(1.0 - normal_cos * normal_cos)
    normals = jnp.stack([sine * jnp.cos(normal_angle), sine * jnp.sin(normal_angle), normal_cos])
    weighted = (node_areas * inverse_four_pi)[None, :] * normals
    sources = jnp.pad(
        jnp.concatenate([surface_points, weighted], axis=0), ((0, 2), (0, PAD_SLOTS - SLOTS))
    )

    def apply(v, pieces):
        ghosts = exchange(pieces)
        own, *back = call(
            apply_kernel, [(OWN_ROWS, LANES)] + [PIECE] * 4, 2,
            (parity, live_blocks, v, *ghosts, conn, grads, vol),
            scratch=[
                pltpu.VMEM((EXT_ROWS, LANES), F32),
                pltpu.VMEM((4, ELEM_ROWS, LANES), F32),
                pltpu.VMEM((EXT_ROWS, LANES), F32),
            ],
        )
        returned = exchange(back)
        new, *out = call(
            combine_kernel, [(OWN_ROWS, LANES)] + [PIECE] * 4, 1,
            (parity, own, *returned, lists, v, mass),
        )
        return new, out

    first = call(pick_kernel, [PIECE] * 4, 1, (parity, b, lists))
    v1, second = apply(b, first)
    v2, third = apply(v1, second)
    ghosts = exchange(third)
    sub = (N_DEV // 4, LANES)
    partial, trace = call(
        far_kernel, [(N_DEV, LANES), (3, 8, LANES)], 2,
        (parity, live_blocks, b, v1, v2, *ghosts, conn, grads, vol, mass, nodes, sources, targets),
        scratch=[pltpu.VMEM((EXT_ROWS, LANES), F32)]
        + [pltpu.VMEM(sub, F32)] * 6
        + [pltpu.VMEM((8, PAD_SLOTS), BF16)],
    )
    got = lax.all_to_all(partial, ("row", "col"), 0, 0, tiled=True)
    potential, dirichlet = call(
        final_kernel, [(OWN_ROWS, LANES), (1, LANES)], 0, (got, b, v1, v2, trace)
    )
    return potential.reshape(NN_DEV), dirichlet[0, :TGT_DEV]


def solution(mesh):
    both = ("row", "col")
    return jax.shard_map(
        per_device,
        mesh=mesh,
        in_specs=(
            P(None, both), P(None, both), P(both), P(both), P(None, both), P(both),
            P(both), P(both), P(None, both), P(both), P(both), P(both),
        ),
        out_specs=(P(both), P(both)),
        check_vma=False,
    )
```

```python
import functools
import math

import jax
import jax.numpy as jnp
from jax import lax
from jax.experimental import pallas as pl
from jax.experimental.pallas import tpu as pltpu
from jax.sharding import PartitionSpec as P

F32 = jnp.float32
BF16 = jnp.bfloat16
LANES = 128
NN_DEV = 2048
NE_DEV = 8192
EBLK = 1024
GH = 256
TGT_DEV = 32
OWN_ROWS = NN_DEV // LANES
GHOST_ROWS = 4 * GH // LANES
EXT_ROWS = OWN_ROWS + GHOST_ROWS
ELEM_ROWS = NE_DEV // LANES
SLOTS = 320
PAD_SLOTS = 384
N_DEV = 256
SPLITS = 3
SCALE = 1.0 / 64.0
VMEM_GRANT = 16 << 20
GROUP = 4
smoothing = 0.0001
inverse_four_pi = 1.0 / (4.0 * math.pi)


def gather_rows(table, index):
    rows = table.shape[0]
    high = index >> 7
    low = index & 127
    out = jnp.zeros(index.shape, F32)
    for r in range(rows):
        row = jnp.broadcast_to(table[r:r + 1, :], index.shape)
        out = jnp.where(high == r, jnp.take_along_axis(row, low, axis=1), out)
    return out


def split_terms(terms):
    parts = []
    rest = terms
    for _ in range(SPLITS):
        part = rest.astype(BF16)
        parts.append(part.astype(F32))
        rest = rest - parts[-1]
    return parts


def scatter_block(index_rows, term_rows, rows):
    sub = lax.broadcasted_iota(jnp.int32, (LANES, LANES), 0)
    sub_rows = lax.broadcasted_iota(jnp.int32, (rows, LANES), 0)
    hot_blocks = []
    weight_blocks = []
    for index, terms in zip(index_rows, term_rows):
        low = jnp.broadcast_to(index & 127, (LANES, LANES))
        hot_blocks.append(jnp.where(sub == low, 1.0, 0.0).astype(BF16))
        mine = sub_rows == jnp.broadcast_to(index >> 7, (rows, LANES))
        pieces = [
            jnp.where(mine, jnp.broadcast_to(part, (rows, LANES)), 0.0)
            for part in split_terms(terms)
        ]
        weight_blocks.append(jnp.concatenate(pieces, axis=0).astype(BF16))
    hot = jnp.concatenate(hot_blocks, axis=1)
    weights = jnp.concatenate(weight_blocks, axis=1)
    total = lax.dot_general(
        weights, hot, (((1,), (1,)), ((), ())), preferred_element_type=F32
    )
    out = total[0:rows]
    for k in range(1, SPLITS):
        out = out + total[k * rows:(k + 1) * rows]
    return out


def element_gradient(ext, conn_ref, grad_ref, t):
    block = pl.ds(pl.multiple_of(t * 8, 8), 8)
    corner = [gather_rows(ext, conn_ref[a, block, :]) for a in range(4)]
    grads = [grad_ref[c, block, :] for c in range(9)]
    base = corner[3]
    diff = [corner[a] - base for a in range(3)]
    field = [
        grads[k] * diff[0] + grads[3 + k] * diff[1] + grads[6 + k] * diff[2]
        for k in range(3)
    ]
    return grads, field


def block_volume(vol_ref, t):
    return vol_ref[pl.ds(pl.multiple_of(t * 8, 8), 8), :]


def extend(parity_ref, v, ghosts):
    first = parity_ref[0] == 0
    second = parity_ref[1] == 0
    row_a, row_b, col_a, col_b = ghosts
    return jnp.concatenate(
        [
            v,
            jnp.where(first, row_b, row_a),
            jnp.where(first, row_a, row_b),
            jnp.where(second, col_b, col_a),
            jnp.where(second, col_a, col_b),
        ],
        axis=0,
    )


def put_outgoing(parity_ref, blocks, out_refs):
    first = parity_ref[0] == 0
    second = parity_ref[1] == 0
    out_refs[0][...] = jnp.where(first, blocks[0], blocks[1])
    out_refs[1][...] = jnp.where(first, blocks[1], blocks[0])
    out_refs[2][...] = jnp.where(second, blocks[2], blocks[3])
    out_refs[3][...] = jnp.where(second, blocks[3], blocks[2])


def blocks_of(rows):
    return [rows[2 * d:2 * d + 2] for d in range(4)]


def pick_kernel(parity_ref, v_ref, list_ref, point_ref, target_ref, *out_refs):
    put_outgoing(parity_ref, blocks_of(gather_rows(v_ref[...], list_ref[...])), out_refs)
    lane = lax.broadcasted_iota(jnp.int32, (1, LANES), 1)
    own = jnp.zeros((1, LANES), F32)
    for c in range(3):
        part = point_ref[c:c + 1, 0:LANES]
        if c:
            part = pltpu.roll(part, TGT_DEV * c, 1)
        own = jnp.where((lane >= TGT_DEV * c) & (lane < TGT_DEV * (c + 1)), part, own)
    target_ref[...] = jnp.broadcast_to(own, (N_DEV, LANES))


def apply_kernel(parity_ref, live_ref, v_ref, ga, gb, gc, gd, conn_ref, grad_ref, vol_ref,
                 own_ref, oa, ob, oc, od, ext_ref, term_ref, acc_ref):
    ext_ref[...] = extend(parity_ref, v_ref[...], [ga[...], gb[...], gc[...], gd[...]])

    def element_block(t, carry):
        ext = ext_ref[...]
        grads, field = element_gradient(ext, conn_ref, grad_ref, t)
        vol = block_volume(vol_ref, t)
        block = pl.ds(pl.multiple_of(t * 8, 8), 8)
        field = [vol * f for f in field]
        last = jnp.zeros_like(vol)
        for a in range(3):
            term = grads[3 * a] * field[0] + grads[3 * a + 1] * field[1] + grads[3 * a + 2] * field[2]
            term_ref[a, block, :] = term
            last = last - term
        term_ref[3, block, :] = last
        return carry

    lax.fori_loop(0, live_ref[0], element_block, 0)
    acc_ref[...] = jnp.zeros_like(acc_ref)

    def scatter_step(t, carry):
        block = pl.ds(pl.multiple_of(t * 8, 8), 8)
        total = acc_ref[...]
        for a in range(4):
            index = conn_ref[a, block, :]
            terms = term_ref[a, block, :]
            total = total + scatter_block(
                [index[s:s + 1] for s in range(8)], [terms[s:s + 1] for s in range(8)], EXT_ROWS
            )
        acc_ref[...] = total
        return carry

    lax.fori_loop(0, live_ref[0], scatter_step, 0)
    own_ref[...] = acc_ref[0:OWN_ROWS, :]
    put_outgoing(parity_ref, swap_pairs(blocks_of(acc_ref[OWN_ROWS:EXT_ROWS, :])), (oa, ob, oc, od))


def swap_pairs(blocks):
    return [blocks[1], blocks[0], blocks[3], blocks[2]]


def combine_kernel(parity_ref, own_ref, ra, rb, rc, rd, list_ref, v_ref, mass_ref,
                   next_ref, oa, ob, oc, od):
    first = parity_ref[0] == 0
    second = parity_ref[1] == 0
    lists = list_ref[...]
    returned = jnp.concatenate(
        [
            jnp.where(first, ra[...], rb[...]),
            jnp.where(first, rb[...], ra[...]),
            jnp.where(second, rc[...], rd[...]),
            jnp.where(second, rd[...], rc[...]),
        ],
        axis=0,
    )
    added = scatter_block(
        [lists[s:s + 1] for s in range(8)], [returned[s:s + 1] for s in range(8)], OWN_ROWS
    )
    value = (mass_ref[...] * v_ref[...] + own_ref[...] + added) * SCALE
    next_ref[...] = value
    put_outgoing(parity_ref, blocks_of(gather_rows(value, lists)), (oa, ob, oc, od))


def far_kernel(parity_ref, live_ref, b_ref, v1_ref, v2_ref, ga, gb, gc, gd, conn_ref, grad_ref, vol_ref,
               mass_ref, node_ref, src_ref, tgt_ref,
               out_ref, trace_ref, ext_ref, tx, ty, tz, d0, d1, d2, lhs_ref, wide_ref, entry_ref):
    b = b_ref[...]
    v1 = v1_ref[...]
    v2 = v2_ref[...]
    ext_ref[...] = extend(parity_ref, v2, [ga[...], gb[...], gc[...], gd[...]])

    def energy_block(t, total):
        ext = ext_ref[...]
        _, field = element_gradient(ext, conn_ref, grad_ref, t)
        vol = block_volume(vol_ref, t)
        return total + vol * (field[0] * field[0] + field[1] * field[1] + field[2] * field[2])

    energy = lax.fori_loop(0, live_ref[0], energy_block, jnp.zeros((8, LANES), F32))
    pairs = [b * b, b * v1, v1 * v1, v1 * v2, v2 * v2, mass_ref[...] * v2 * v2]
    sums = [p[0:8] + p[8:16] for p in pairs]
    sums[5] = (sums[5] + energy) * SCALE
    sub = lax.broadcasted_iota(jnp.int32, (8, LANES), 0)
    lane_row = lax.broadcasted_iota(jnp.int32, (1, LANES), 1)
    moments = jnp.zeros((1, LANES), F32)
    for k in range(6):
        moments = jnp.where(lane_row == 96 + k, jnp.sum(sums[k]), moments)

    nodes = node_ref[...]
    traces = [gather_rows(table, nodes) for table in (b, v1, v2)]
    for k in range(3):
        trace_ref[k] = traces[k]
    slot = lax.broadcasted_iota(jnp.int32, (8, LANES), 0) * LANES + lax.broadcasted_iota(jnp.int32, (8, LANES), 1)
    for r in range(PAD_SLOTS // LANES):
        block = jnp.zeros((8, LANES), F32)
        for k in range(3):
            t = jnp.where(slot < SLOTS, traces[k], 0.0)[r:r + 1, :]
            high = t.astype(BF16).astype(F32)
            block = jnp.where(sub == 2 * k, high, block)
            block = jnp.where(sub == 2 * k + 1, t - high, block)
        lhs_ref[:, r * LANES:(r + 1) * LANES] = block.astype(BF16)

    lane = lax.broadcasted_iota(jnp.int32, (N_DEV // 4, LANES), 1)
    for c, ref in enumerate((tx, ty, tz)):
        out = jnp.zeros((N_DEV // 4, LANES), F32)
        for j in range(4):
            part = tgt_ref[pl.ds(j, N_DEV // 4, stride=4), :]
            shift = (32 * j - 32 * c) % LANES
            if shift:
                part = pltpu.roll(part, shift, 1)
            out = jnp.where((lane >= 32 * j) & (lane < 32 * j + 32), part, out)
        ref[...] = out

    cols = jnp.transpose(src_ref[...])
    for c in range(6):
        wide_ref[c] = jnp.broadcast_to(cols[:, c:c + 1], (PAD_SLOTS, LANES))
    entry_ref[SLOTS:PAD_SLOTS, :] = jnp.zeros((PAD_SLOTS - SLOTS, GROUP * LANES), BF16)

    def target_group(g, carry):
        first = g * GROUP
        for s in range(SLOTS // 16):
            rows = slice(16 * s, 16 * s + 16)
            sx, sy, sz, wx, wy, wz = [wide_ref[c, rows, :] for c in range(6)]
            for q in range(GROUP):
                at = pl.ds(first + q, 1)
                dx = tx[at, :] - sx
                dy = ty[at, :] - sy
                dz = tz[at, :] - sz
                radius_sq = dx * dx + dy * dy + dz * dz + smoothing
                inverse = lax.rsqrt(radius_sq)
                numerator = dx * wx + dy * wy + dz * wz
                entry_ref[rows, q * LANES:(q + 1) * LANES] = (
                    numerator * (inverse * inverse * inverse)
                ).astype(BF16)
        res = jnp.dot(lhs_ref[...], entry_ref[...], preferred_element_type=F32)
        for q in range(GROUP):
            at = pl.ds(first + q, 1)
            part = res[:, q * LANES:(q + 1) * LANES]
            d0[at, :] = part[0:1] + part[1:2]
            d1[at, :] = part[2:3] + part[3:4]
            d2[at, :] = part[4:5] + part[5:6]
        return carry

    lax.fori_loop(0, N_DEV // 4 // GROUP, target_group, 0)
    spread = jnp.broadcast_to(moments, (N_DEV // 4, LANES))
    for j in range(4):
        out = spread
        for k, ref in enumerate((d0, d1, d2)):
            part = ref[...]
            shift = (32 * k - 32 * j) % LANES
            if shift:
                part = pltpu.roll(part, shift, 1)
            out = jnp.where((lane >= 32 * k) & (lane < 32 * k + 32), part, out)
        out_ref[pl.ds(j, N_DEV // 4, stride=4), :] = out


def final_kernel(got_ref, b_ref, v1_ref, v2_ref, trace_ref, pot_ref, dir_ref):
    total = jnp.sum(got_ref[...], axis=0, keepdims=True)
    lane = lax.broadcasted_iota(jnp.int32, (1, LANES), 1)
    m = [jnp.sum(jnp.where(lane == 96 + k, total, 0.0), axis=1, keepdims=True) for k in range(6)]
    l1 = m[2] / m[1]
    l2 = m[3] / m[1]
    s11 = m[3] - l1 * m[2]
    s12 = m[4] - l1 * m[3]
    s22 = m[5] - l2 * m[3]
    y1 = m[1] - l1 * m[0]
    y2 = m[2] - l2 * m[0]
    keep1 = s11 > 4e-7 * m[3]
    safe11 = jnp.where(keep1, s11, 1.0)
    ratio = jnp.where(keep1, s12 / safe11, 0.0)
    d2 = s22 - ratio * s12
    keep2 = keep1 & (d2 > 4e-7 * m[5])
    c2 = jnp.where(keep2, (y2 - ratio * y1) / jnp.where(keep2, d2, 1.0), 0.0)
    c1 = jnp.where(keep1, (y1 - s12 * c2) / safe11, 0.0)
    c0 = (m[0] - m[2] * c1 - m[3] * c2) / m[1]
    c0 = c0 * SCALE
    c1 = c1 * SCALE
    c2 = c2 * SCALE
    pot_ref[...] = c0 * b_ref[...] + c1 * v1_ref[...] + c2 * v2_ref[...]
    out = jnp.zeros((1, LANES), F32)
    for k, c in enumerate((c0, c1, c2)):
        part = total
        if k:
            part = pltpu.roll(total, LANES - 32 * k, 1)
        out = out + c * (part - 0.5 * trace_ref[k, 0:1, :])
    dir_ref[...] = out[:, 0:TGT_DEV]


def call(body, out_shapes, smem, args, scratch=(), flops=1000000):
    specs = [pl.BlockSpec(memory_space=pltpu.SMEM)] * smem
    specs += [pl.BlockSpec(memory_space=pltpu.VMEM)] * (len(args) - smem)
    return pl.pallas_call(
        body,
        out_shape=[jax.ShapeDtypeStruct(s, F32) for s in out_shapes],
        in_specs=specs,
        out_specs=[pl.BlockSpec(memory_space=pltpu.VMEM)] * len(out_shapes),
        scratch_shapes=list(scratch),
        compiler_params=pltpu.CompilerParams(vmem_limit_bytes=VMEM_GRANT),
    )(*args)


PIECE = (2, LANES)


def pairs(count, start):
    out = []
    for i in range(start, count - 1, 2):
        out += [(i, i + 1), (i + 1, i)]
    return out


def exchange(pieces):
    rows = lax.axis_size("row")
    cols = lax.axis_size("col")
    row_a = lax.ppermute(pieces[0], "row", pairs(rows, 0))
    col_a = lax.ppermute(pieces[2], "col", pairs(cols, 0))
    row_b = lax.ppermute(pieces[1], "row", pairs(rows, 1))
    col_b = lax.ppermute(pieces[3], "col", pairs(cols, 1))
    return [row_a, row_b, col_a, col_b]


def per_device(connectivity, gradients, volumes, live_blocks, send_lists, divergence, mass_shift,
               boundary_nodes, surface_points, normal_cos, normal_angle, node_areas):
    parity = jnp.stack([lax.axis_index("row") % 2, lax.axis_index("col") % 2]).astype(jnp.int32)
    conn = connectivity.reshape(4, ELEM_ROWS, LANES)
    grads = gradients.reshape(9, ELEM_ROWS, LANES)
    vol = volumes.reshape(ELEM_ROWS, LANES)
    lists = send_lists.reshape(4 * GH // LANES, LANES)
    b = divergence.reshape(OWN_ROWS, LANES)
    mass = mass_shift.reshape(OWN_ROWS, LANES)
    nodes = jnp.pad(boundary_nodes, (0, 8 * LANES - SLOTS)).reshape(8, LANES)

    sine = jnp.sqrt(1.0 - normal_cos * normal_cos)
    normals = jnp.stack([sine * jnp.cos(normal_angle), sine * jnp.sin(normal_angle), normal_cos])
    weighted = (node_areas * inverse_four_pi)[None, :] * normals
    sources = jnp.pad(
        jnp.concatenate([surface_points, weighted], axis=0), ((0, 2), (0, PAD_SLOTS - SLOTS))
    )

    def apply(v, pieces):
        ghosts = exchange(pieces)
        own, *back = call(
            apply_kernel, [(OWN_ROWS, LANES)] + [PIECE] * 4, 2,
            (parity, live_blocks, v, *ghosts, conn, grads, vol),
            scratch=[
                pltpu.VMEM((EXT_ROWS, LANES), F32),
                pltpu.VMEM((4, ELEM_ROWS, LANES), F32),
                pltpu.VMEM((EXT_ROWS, LANES), F32),
            ],
        )
        returned = exchange(back)
        new, *out = call(
            combine_kernel, [(OWN_ROWS, LANES)] + [PIECE] * 4, 1,
            (parity, own, *returned, lists, v, mass),
        )
        return new, out

    mine, *first = call(
        pick_kernel, [(N_DEV, LANES)] + [PIECE] * 4, 1, (parity, b, lists, surface_points)
    )
    targets = lax.all_to_all(mine, ("row", "col"), 0, 0, tiled=True)
    v1, second = apply(b, first)
    v2, third = apply(v1, second)
    ghosts = exchange(third)
    sub = (N_DEV // 4, LANES)
    partial, trace = call(
        far_kernel, [(N_DEV, LANES), (3, 8, LANES)], 2,
        (parity, live_blocks, b, v1, v2, *ghosts, conn, grads, vol, mass, nodes, sources, targets),
        scratch=[pltpu.VMEM((EXT_ROWS, LANES), F32)]
        + [pltpu.VMEM(sub, F32)] * 6
        + [
            pltpu.VMEM((8, PAD_SLOTS), BF16),
            pltpu.VMEM((6, PAD_SLOTS, LANES), F32),
            pltpu.VMEM((PAD_SLOTS, GROUP * LANES), BF16),
        ],
    )
    got = lax.all_to_all(partial, ("row", "col"), 0, 0, tiled=True)
    potential, dirichlet = call(
        final_kernel, [(OWN_ROWS, LANES), (1, TGT_DEV)], 0, (got, b, v1, v2, trace)
    )
    return potential.reshape(NN_DEV), dirichlet.reshape(TGT_DEV)


def solution(mesh):
    both = ("row", "col")
    return jax.shard_map(
        per_device,
        mesh=mesh,
        in_specs=(
            P(None, both), P(None, both), P(both), P(both), P(None, both), P(both),
            P(both), P(both), P(None, both), P(both), P(both), P(both),
        ),
        out_specs=(P(both), P(both)),
        check_vma=False,
    )
```

```python
import math

import jax
import jax.numpy as jnp
from jax import lax
from jax.experimental import pallas as pl
from jax.experimental.pallas import tpu as pltpu
from jax.sharding import PartitionSpec as P


F32 = jnp.float32
BF16 = jnp.bfloat16
LANES = 128
NN_DEV = 2048
GH = 256
TGT_DEV = 32
OWN_ROWS = NN_DEV // LANES
EXT_ROWS = OWN_ROWS + 4 * GH // LANES
HIGH_ROWS = 32
ELEM_ROWS = 64
SLOTS = 320
PAD_SLOTS = 384
N_DEV = 256
TGT_ROWS = N_DEV // 4
CHUNKS = 4
GROUP = 4
KDIM = 32
SPLITS = 3
SCALE = 1.0 / 64.0
VMEM_GRANT = 16 << 20
smoothing = 0.0001
inverse_four_pi = 1.0 / (4.0 * math.pi)


def gather_rows(table, index):
    high = index >> 7
    low = index & 127
    out = jnp.zeros(index.shape, F32)
    for r in range(table.shape[0]):
        row = jnp.broadcast_to(table[r:r + 1, :], index.shape)
        out = jnp.where(high == r, jnp.take_along_axis(row, low, axis=1), out)
    return out


def split_terms(terms, count=SPLITS):
    parts = []
    for _ in range(count):
        parts.append(terms.astype(BF16))
        terms = terms - parts[-1].astype(F32)
    return parts


def scatter_block(index, terms, rows):
    rows = -(-rows // 16) * 16
    sub = lax.broadcasted_iota(jnp.int32, (LANES, LANES), 0).astype(F32).astype(BF16)
    sub_rows = lax.broadcasted_iota(jnp.int32, (rows, LANES), 0).astype(F32).astype(BF16)
    one = jnp.ones((LANES, LANES), BF16)
    zero = jnp.zeros((LANES, LANES), BF16)
    zero_rows = jnp.zeros((rows, LANES), BF16)
    low = (index & 127).astype(F32)
    high = (index >> 7).astype(F32)
    parts = [p.astype(F32) for p in split_terms(terms)]
    hot_blocks = []
    weight_blocks = []
    for s in range(8):
        at = slice(s, s + 1)
        low_row = jnp.broadcast_to(low[at], (LANES, LANES)).astype(BF16)
        hot_blocks.append(jnp.where(sub == low_row, one, zero))
        mine = sub_rows == jnp.broadcast_to(high[at], (rows, LANES)).astype(BF16)
        weight_blocks.append(jnp.concatenate(
            [jnp.where(mine, jnp.broadcast_to(p[at], (rows, LANES)).astype(BF16), zero_rows) for p in parts],
            axis=0,
        ))
    total = lax.dot_general(
        jnp.concatenate(weight_blocks, axis=1), jnp.concatenate(hot_blocks, axis=1),
        (((1,), (1,)), ((), ())), preferred_element_type=F32,
    )
    out = total[0:rows]
    for k in range(1, SPLITS):
        out = out + total[k * rows:(k + 1) * rows]
    return out


def conn_block(conn_ref, a, t):
    return conn_ref[pl.ds(32 * t + a, 8, stride=4), :]


def element_gradient(ext, conn_ref, grad_ref, last_ref, t):
    corner = [gather_rows(ext, conn_block(conn_ref, a, t)) for a in range(4)]
    grads = [grad_ref[pl.ds(64 * t + c, 8, stride=8), :] for c in range(8)]
    grads.append(last_ref[pl.ds(pl.multiple_of(8 * t, 8), 8), :])
    diff = [corner[a] - corner[3] for a in range(3)]
    field = [
        grads[k] * diff[0] + grads[3 + k] * diff[1] + grads[6 + k] * diff[2]
        for k in range(3)
    ]
    return grads, field


def block_volume(vol_ref, t):
    return vol_ref[pl.ds(pl.multiple_of(t * 8, 8), 8), :]


def odd(axis):
    return lax.rem(lax.axis_index(axis), 2) == 1


def inside(axis):
    me = lax.axis_index(axis)
    return (me > 0) & (me < lax.axis_size(axis) - 1)


def from_swaps(pieces):
    row_a, row_b, col_a, col_b = [p[...] for p in pieces]
    row_b = jnp.where(inside("row"), row_b, 0.0)
    col_b = jnp.where(inside("col"), col_b, 0.0)
    row_odd = odd("row")
    col_odd = odd("col")
    return [
        jnp.where(row_odd, row_b, row_a),
        jnp.where(row_odd, row_a, row_b),
        jnp.where(col_odd, col_b, col_a),
        jnp.where(col_odd, col_a, col_b),
    ]


def put_outgoing(blocks, out_refs):
    row_odd = odd("row")
    col_odd = odd("col")
    out_refs[0][...] = jnp.where(row_odd, blocks[1], blocks[0])
    out_refs[1][...] = jnp.where(row_odd, blocks[0], blocks[1])
    out_refs[2][...] = jnp.where(col_odd, blocks[3], blocks[2])
    out_refs[3][...] = jnp.where(col_odd, blocks[2], blocks[3])


def extend(v, pieces):
    up, down, right, left = from_swaps(pieces)
    return jnp.concatenate([v, down, up, left, right], axis=0)


def picked_blocks(v, lists):
    got = gather_rows(v, lists)
    return [jnp.concatenate([got[d:d + 1], got[4 + d:5 + d]], axis=0) for d in range(4)]


def pick_kernel(v_ref, list_ref, point_ref, target_ref, *out_refs):
    put_outgoing(picked_blocks(v_ref[...], list_ref[...]), out_refs)
    lane = lax.broadcasted_iota(jnp.int32, (1, LANES), 1)
    own = jnp.zeros((1, LANES), F32)
    for c in range(3):
        part = point_ref[c:c + 1, 0:LANES]
        if c:
            part = pltpu.roll(part, TGT_DEV * c, 1)
        own = jnp.where((lane >= TGT_DEV * c) & (lane < TGT_DEV * (c + 1)), part, own)
    target_ref[...] = jnp.broadcast_to(own, (N_DEV, LANES))


def apply_kernel(live_ref, v_ref, ga, gb, gc, gd, conn_ref, grad_ref, last_ref, vol_ref,
                 own_ref, oa, ob, oc, od, ext_ref, acc_ref):
    ext_ref[...] = extend(v_ref[...], [ga, gb, gc, gd])
    acc_ref[...] = jnp.zeros_like(acc_ref)

    def element_block(t, carry):
        grads, field = element_gradient(ext_ref[...], conn_ref, grad_ref, last_ref, t)
        vol = block_volume(vol_ref, t)
        field = [vol * f for f in field]
        terms = [
            grads[3 * a] * field[0] + grads[3 * a + 1] * field[1] + grads[3 * a + 2] * field[2]
            for a in range(3)
        ]
        terms.append(-(terms[0] + terms[1] + terms[2]))
        total = acc_ref[...]
        for a in range(4):
            total = total + scatter_block(conn_block(conn_ref, a, t), terms[a], EXT_ROWS)
        acc_ref[...] = total
        return carry

    lax.fori_loop(0, live_ref[0], element_block, 0)
    own_ref[...] = acc_ref[0:OWN_ROWS, :]
    down, up, left, right = [
        acc_ref[OWN_ROWS + 2 * d:OWN_ROWS + 2 * d + 2, :] for d in range(4)
    ]
    put_outgoing([up, down, right, left], (oa, ob, oc, od))


def combine_kernel(own_ref, ra, rb, rc, rd, list_ref, v_ref, mass_ref,
                   next_ref, oa, ob, oc, od):
    lists = list_ref[...]
    back = from_swaps([ra, rb, rc, rd])
    terms = jnp.concatenate([b[0:1] for b in back] + [b[1:2] for b in back], axis=0)
    added = scatter_block(lists, terms, OWN_ROWS)
    value = (mass_ref[...] * v_ref[...] + own_ref[...] + added) * SCALE
    next_ref[...] = value
    put_outgoing(picked_blocks(value, lists), (oa, ob, oc, od))


def prepare_kernel(src_ref, tgt_ref, wide_ref, left_ref, right_ref, row_ref):
    src = src_ref[...]
    cols = jnp.transpose(src)
    for c in range(6):
        wide_ref[c] = jnp.broadcast_to(cols[0:SLOTS, c:c + 1], (SLOTS, LANES))
    lane = lax.broadcasted_iota(jnp.int32, (TGT_ROWS, LANES), 1)
    for c in range(3):
        out = jnp.zeros((TGT_ROWS, LANES), F32)
        for j in range(4):
            part = tgt_ref[pl.ds(j, TGT_ROWS, stride=4), :]
            shift = (32 * j - 32 * c) % LANES
            if shift:
                part = pltpu.roll(part, shift, 1)
            out = jnp.where((lane >= 32 * j) & (lane < 32 * j + 32), part, out)
        row_ref[c] = out

    def factors(points, scale, extra, swap):
        norm = points[0] * points[0] + points[1] * points[1] + points[2] * points[2] + extra
        ones = jnp.ones_like(norm)
        lines = []
        for p in points:
            a = [q.astype(F32) for q in split_terms(p * scale)]
            order = (0, 1, 0, 1, 2, 0) if swap else (0, 0, 1, 1, 0, 2)
            lines += [a[k] for k in order]
        norms = [q.astype(F32) for q in split_terms(norm)]
        lines += [ones] * 3 + norms if swap else norms + [ones] * 3
        return lines

    left = factors([src[c:c + 1, :] - 0.5 for c in range(3)], 1.0, 0.0, False)
    left = jnp.concatenate(left + [jnp.zeros((KDIM - 24, PAD_SLOTS), F32)], axis=0)
    left_ref[...] = jnp.transpose(left)[0:SLOTS, :].astype(BF16)
    right = factors([row_ref[c] - 0.5 for c in range(3)], -2.0, smoothing, True)
    zero = jnp.zeros((1, LANES), F32)
    for g in range(TGT_ROWS):
        block = jnp.concatenate([r[g:g + 1, :] for r in right] + [zero] * (KDIM - 24), axis=0)
        right_ref[:, g * LANES:(g + 1) * LANES] = block.astype(BF16)


def entries_kernel(chunk, wide_ref, left_ref, right_ref, row_ref, entry_ref):
    base = chunk * (TGT_ROWS // CHUNKS)

    def target_group(g, carry):
        first = base + g * GROUP
        lanes = pl.ds(pl.multiple_of(first * LANES, GROUP * LANES), GROUP * LANES)
        square = jnp.dot(left_ref[...], right_ref[:, lanes], preferred_element_type=F32)
        for s in range(SLOTS // 16):
            rows = slice(16 * s, 16 * s + 16)
            sx, sy, sz, wx, wy, wz = [wide_ref[c, rows, :] for c in range(6)]
            for q in range(GROUP):
                at = pl.ds(first + q, 1)
                inverse = lax.rsqrt(square[rows, q * LANES:(q + 1) * LANES])
                numerator = (
                    (row_ref[0, at, :] - sx) * wx
                    + (row_ref[1, at, :] - sy) * wy
                    + (row_ref[2, at, :] - sz) * wz
                )
                value = (numerator * (inverse * inverse * inverse)).astype(BF16)
                out = pl.ds(pl.multiple_of((g * GROUP + q) * LANES, LANES), LANES)
                entry_ref[rows, out] = value
        return carry

    lax.fori_loop(0, TGT_ROWS // CHUNKS // GROUP, target_group, 0)


def far_kernel(live_ref, b_ref, v1_ref, v2_ref, ga, gb, gc, gd, conn_ref, grad_ref, last_ref, vol_ref,
               mass_ref, node_ref, e0, e1, e2, e3,
               out_ref, trace_ref, ext_ref, d0, d1, d2, lhs_ref):
    b = b_ref[...]
    v1 = v1_ref[...]
    v2 = v2_ref[...]
    ext_ref[...] = extend(v2, [ga, gb, gc, gd])

    def energy_block(t, total):
        _, field = element_gradient(ext_ref[...], conn_ref, grad_ref, last_ref, t)
        return total + block_volume(vol_ref, t) * (
            field[0] * field[0] + field[1] * field[1] + field[2] * field[2]
        )

    energy = lax.fori_loop(0, live_ref[0], energy_block, jnp.zeros((8, LANES), F32))
    products = [b * b, b * v1, v1 * v1, v1 * v2, v2 * v2, mass_ref[...] * v2 * v2]
    sums = [p[0:8] + p[8:16] for p in products]
    sums[5] = (sums[5] + energy) * SCALE
    sub = lax.broadcasted_iota(jnp.int32, (8, LANES), 0)
    lane_row = lax.broadcasted_iota(jnp.int32, (1, LANES), 1)
    moments = jnp.zeros((1, LANES), F32)
    for k in range(6):
        moments = jnp.where(lane_row == 96 + k, jnp.sum(sums[k]), moments)

    nodes = node_ref[...]
    traces = [gather_rows(table, nodes) for table in (b, v1, v2)]
    for k in range(3):
        trace_ref[k] = traces[k]
    for r in range(PAD_SLOTS // LANES):
        block = jnp.zeros((8, LANES), F32)
        for k in range(3):
            t = traces[k][r:r + 1, :]
            high = t.astype(BF16).astype(F32)
            block = jnp.where(sub == 2 * k, high, block)
            block = jnp.where(sub == 2 * k + 1, t - high, block)
        lhs_ref[:, r * LANES:(r + 1) * LANES] = block.astype(BF16)
    lhs = lhs_ref[:, 0:SLOTS]
    each = TGT_ROWS // CHUNKS
    for chunk, entry_ref in enumerate((e0, e1, e2, e3)):
        res = jnp.dot(lhs, entry_ref[...], preferred_element_type=F32)
        for q in range(each):
            at = slice(chunk * each + q, chunk * each + q + 1)
            part = res[:, q * LANES:(q + 1) * LANES]
            d0[at, :] = part[0:1] + part[1:2]
            d1[at, :] = part[2:3] + part[3:4]
            d2[at, :] = part[4:5] + part[5:6]

    lane = lax.broadcasted_iota(jnp.int32, (TGT_ROWS, LANES), 1)
    spread = jnp.broadcast_to(moments, (TGT_ROWS, LANES))
    for j in range(4):
        out = spread
        for k, ref in enumerate((d0, d1, d2)):
            part = ref[...]
            shift = (32 * k - 32 * j) % LANES
            if shift:
                part = pltpu.roll(part, shift, 1)
            out = jnp.where((lane >= 32 * k) & (lane < 32 * k + 32), part, out)
        out_ref[pl.ds(j, TGT_ROWS, stride=4), :] = out


def final_kernel(got_ref, b_ref, v1_ref, v2_ref, trace_ref, pot_ref, dir_ref):
    total = jnp.sum(got_ref[...], axis=0, keepdims=True)
    lane = lax.broadcasted_iota(jnp.int32, (1, LANES), 1)
    m = [jnp.sum(jnp.where(lane == 96 + k, total, 0.0), axis=1, keepdims=True) for k in range(6)]
    l1 = m[2] / m[1]
    l2 = m[3] / m[1]
    s11 = m[3] - l1 * m[2]
    s12 = m[4] - l1 * m[3]
    s22 = m[5] - l2 * m[3]
    y1 = m[1] - l1 * m[0]
    y2 = m[2] - l2 * m[0]
    keep1 = s11 > 4e-7 * m[3]
    safe11 = jnp.where(keep1, s11, 1.0)
    ratio = jnp.where(keep1, s12 / safe11, 0.0)
    d2 = s22 - ratio * s12
    keep2 = keep1 & (d2 > 4e-7 * m[5])
    c2 = jnp.where(keep2, (y2 - ratio * y1) / jnp.where(keep2, d2, 1.0), 0.0)
    c1 = jnp.where(keep1, (y1 - s12 * c2) / safe11, 0.0)
    c0 = (m[0] - m[2] * c1 - m[3] * c2) / m[1]
    c0 = c0 * SCALE
    c1 = c1 * SCALE
    c2 = c2 * SCALE
    pot_ref[...] = c0 * b_ref[...] + c1 * v1_ref[...] + c2 * v2_ref[...]
    out = jnp.zeros((1, LANES), F32)
    for k, c in enumerate((c0, c1, c2)):
        part = total
        if k:
            part = pltpu.roll(total, LANES - 32 * k, 1)
        out = out + c * (part - 0.5 * trace_ref[k, 0:1, :])
    dir_ref[...] = out[:, 0:TGT_DEV]


def call(body, out_shapes, args, smem=0, scratch=(), cost=2000000):
    specs = [pl.BlockSpec(memory_space=pltpu.SMEM)] * smem
    specs += [pl.BlockSpec(memory_space=pltpu.VMEM)] * (len(args) - smem)
    out_shapes = [o if isinstance(o, jax.ShapeDtypeStruct) else jax.ShapeDtypeStruct(o, F32) for o in out_shapes]
    return pl.pallas_call(
        body,
        out_shape=out_shapes,
        in_specs=specs,
        out_specs=[pl.BlockSpec(memory_space=pltpu.VMEM)] * len(out_shapes),
        scratch_shapes=list(scratch),
        compiler_params=pltpu.CompilerParams(vmem_limit_bytes=VMEM_GRANT),
        cost_estimate=pl.CostEstimate(flops=cost, bytes_accessed=1 << 20, transcendentals=0),
    )(*args)


PIECE = (2, LANES)


def first_pairs(count):
    return [(i, i ^ 1) for i in range(count)]


def second_pairs(count):
    return [(i, (((i + 1) ^ 1) - 1) % count) for i in range(count)]


def exchange(pieces):
    rows = lax.axis_size("row")
    cols = lax.axis_size("col")
    row_a = lax.ppermute(pieces[0], "row", first_pairs(rows))
    col_a = lax.ppermute(pieces[2], "col", first_pairs(cols))
    row_b = lax.ppermute(pieces[1], "row", second_pairs(rows))
    col_b = lax.ppermute(pieces[3], "col", second_pairs(cols))
    return [row_a, row_b, col_a, col_b]


def per_device(connectivity, gradients, volumes, live_blocks, send_lists, divergence, mass_shift,
               boundary_nodes, surface_points, normal_cos, normal_angle, node_areas):
    conn = connectivity.reshape(4, ELEM_ROWS, LANES).transpose(1, 0, 2).reshape(4 * ELEM_ROWS, LANES)
    grads = gradients[0:8].reshape(8, ELEM_ROWS, LANES).transpose(1, 0, 2).reshape(8 * ELEM_ROWS, LANES)
    last = gradients[8].reshape(ELEM_ROWS, LANES)
    vol = volumes.reshape(ELEM_ROWS, LANES)
    lists = send_lists.reshape(4, 2, LANES).transpose(1, 0, 2).reshape(8, LANES)
    b = divergence.reshape(OWN_ROWS, LANES)
    mass = mass_shift.reshape(OWN_ROWS, LANES)
    nodes = jnp.pad(boundary_nodes, (0, 8 * LANES - SLOTS)).reshape(8, LANES)
    elements = (conn, grads, last, vol)

    mine, *pieces = call(pick_kernel, [(N_DEV, LANES)] + [PIECE] * 4, (b, lists, surface_points))
    targets = lax.all_to_all(mine, ("row", "col"), 0, 0, tiled=True)
    sine = jnp.sqrt(1.0 - normal_cos * normal_cos)
    normals = jnp.stack([sine * jnp.cos(normal_angle), sine * jnp.sin(normal_angle), normal_cos])
    weighted = (node_areas * inverse_four_pi)[None, :] * normals
    sources = jnp.pad(
        jnp.concatenate([surface_points, weighted], axis=0), ((0, 2), (0, PAD_SLOTS - SLOTS))
    )
    prepared = None
    chunks = []

    def fill():
        nonlocal prepared
        if prepared is None:
            prepared = call(
                prepare_kernel,
                [
                    (6, SLOTS, LANES),
                    jax.ShapeDtypeStruct((SLOTS, KDIM), BF16),
                    jax.ShapeDtypeStruct((KDIM, TGT_ROWS * LANES), BF16),
                    (3, TGT_ROWS, LANES),
                ],
                (sources, targets),
            )
        chunk = len(chunks)
        chunks.append(call(
            lambda *refs: entries_kernel(chunk, *refs),
            [jax.ShapeDtypeStruct((SLOTS, TGT_ROWS // CHUNKS * LANES), BF16)],
            prepared,
        )[0])

    def swap(number, pieces):
        out = exchange(pieces)
        if number:
            fill()
        return out

    vectors = [b]
    for step in range(2):
        ghosts = swap(2 * step, pieces)
        own, *back = call(
            apply_kernel, [(OWN_ROWS, LANES)] + [PIECE] * 4,
            (live_blocks, vectors[-1], *ghosts, *elements), smem=1,
            scratch=[pltpu.VMEM((EXT_ROWS, LANES), F32), pltpu.VMEM((HIGH_ROWS, LANES), F32)],
        )
        returned = swap(2 * step + 1, back)
        new, *pieces = call(
            combine_kernel, [(OWN_ROWS, LANES)] + [PIECE] * 4,
            (own, *returned, lists, vectors[-1], mass),
        )
        vectors.append(new)
    ghosts = swap(4, pieces)
    partial, trace = call(
        far_kernel, [(N_DEV, LANES), (3, 8, LANES)],
        (live_blocks, *vectors, *ghosts, *elements, mass, nodes, *chunks), smem=1,
        scratch=[pltpu.VMEM((EXT_ROWS, LANES), F32)]
        + [pltpu.VMEM((TGT_ROWS, LANES), F32)] * 3
        + [pltpu.VMEM((8, PAD_SLOTS), BF16)],
    )
    got = lax.all_to_all(partial, ("row", "col"), 0, 0, tiled=True)
    potential, dirichlet = call(
        final_kernel, [(OWN_ROWS, LANES), (1, TGT_DEV)], (got, *vectors, trace)
    )
    return potential.reshape(NN_DEV), dirichlet.reshape(TGT_DEV)


def solution(mesh):
    both = ("row", "col")

    return jax.shard_map(
        per_device,
        mesh=mesh,
        in_specs=(
            P(None, both), P(None, both), P(both), P(both), P(None, both), P(both),
            P(both), P(both), P(None, both), P(both), P(both), P(both),
        ),
        out_specs=(P(both), P(both)),
        check_vma=False,
    )
```

```python
import math

import jax
import jax.numpy as jnp
from jax import lax
from jax.experimental import pallas as pl
from jax.experimental.pallas import tpu as pltpu
from jax.sharding import PartitionSpec as P


F32 = jnp.float32
BF16 = jnp.bfloat16
LANES = 128
NN_DEV = 2048
EBLK = 1024
GH = 256
TGT_DEV = 32
OWN_ROWS = NN_DEV // LANES
EXT_ROWS = OWN_ROWS + 4 * GH // LANES
HIGH_ROWS = 32
ELEM_ROWS = 64
SLOTS = 320
PAD_SLOTS = 384
N_DEV = 256
TGT_ROWS = N_DEV // 4
CHUNKS = (20, 24, 20)
GROUP = 4
KDIM = 32
SPLITS = 3
SCALE = 1.0 / 64.0
VMEM_GRANT = 16 << 20
smoothing = 0.0001
inverse_four_pi = 1.0 / (4.0 * math.pi)


def gather_rows(table, index):
    high = index >> 7
    low = index & 127
    out = jnp.zeros(index.shape, F32)
    for r in range(table.shape[0]):
        row = jnp.broadcast_to(table[r:r + 1, :], index.shape)
        out = jnp.where(high == r, jnp.take_along_axis(row, low, axis=1), out)
    return out


def split_terms(terms, count=SPLITS):
    parts = []
    for _ in range(count):
        parts.append(terms.astype(BF16))
        terms = terms - parts[-1].astype(F32)
    return parts


def scatter_block(index, terms, rows):
    rows = -(-rows // 16) * 16
    sub = lax.broadcasted_iota(jnp.int32, (LANES, LANES), 0).astype(F32).astype(BF16)
    sub_rows = lax.broadcasted_iota(jnp.int32, (rows, LANES), 0).astype(F32).astype(BF16)
    one = jnp.ones((LANES, LANES), BF16)
    zero = jnp.zeros((LANES, LANES), BF16)
    zero_rows = jnp.zeros((rows, LANES), BF16)
    low = (index & 127).astype(F32)
    high = (index >> 7).astype(F32)
    parts = [p.astype(F32) for p in split_terms(terms)]
    hot_blocks = []
    weight_blocks = []
    for s in range(8):
        at = slice(s, s + 1)
        low_row = jnp.broadcast_to(low[at], (LANES, LANES)).astype(BF16)
        hot_blocks.append(jnp.where(sub == low_row, one, zero))
        mine = sub_rows == jnp.broadcast_to(high[at], (rows, LANES)).astype(BF16)
        weight_blocks.append(jnp.concatenate(
            [jnp.where(mine, jnp.broadcast_to(p[at], (rows, LANES)).astype(BF16), zero_rows) for p in parts],
            axis=0,
        ))
    total = lax.dot_general(
        jnp.concatenate(weight_blocks, axis=1), jnp.concatenate(hot_blocks, axis=1),
        (((1,), (1,)), ((), ())), preferred_element_type=F32,
    )
    out = total[0:rows]
    for k in range(1, SPLITS):
        out = out + total[k * rows:(k + 1) * rows]
    return out


def conn_block(conn_ref, a, t):
    return conn_ref[pl.ds(32 * t + a, 8, stride=4), :]


def element_gradient(ext, conn_ref, grad_ref, turn_ref, t):
    corner = [gather_rows(ext, conn_block(conn_ref, a, t)) for a in range(4)]
    for k in range(8):
        lanes = pl.ds(pl.multiple_of(EBLK * t + LANES * k, LANES), LANES)
        turn_ref[8 * k:8 * k + 8, :] = grad_ref[0:8, lanes]
        turn_ref[64 + k:65 + k, :] = grad_ref[8:9, lanes]
    grads = [turn_ref[pl.ds(c, 8, stride=8), :] for c in range(8)] + [turn_ref[64:72, :]]
    diff = [corner[a] - corner[3] for a in range(3)]
    field = [
        grads[k] * diff[0] + grads[3 + k] * diff[1] + grads[6 + k] * diff[2]
        for k in range(3)
    ]
    return grads, field


def block_volume(vol_ref, t):
    return vol_ref[pl.ds(pl.multiple_of(t * 8, 8), 8), :]


def odd(axis):
    return lax.rem(lax.axis_index(axis), 2) == 1


def inside(axis):
    me = lax.axis_index(axis)
    return (me > 0) & (me < lax.axis_size(axis) - 1)


def from_swaps(pieces):
    row_a, row_b, col_a, col_b = [p[...] for p in pieces]
    row_b = jnp.where(inside("row"), row_b, 0.0)
    col_b = jnp.where(inside("col"), col_b, 0.0)
    row_odd = odd("row")
    col_odd = odd("col")
    return [
        jnp.where(row_odd, row_b, row_a),
        jnp.where(row_odd, row_a, row_b),
        jnp.where(col_odd, col_b, col_a),
        jnp.where(col_odd, col_a, col_b),
    ]


def put_outgoing(blocks, out_refs):
    row_odd = odd("row")
    col_odd = odd("col")
    out_refs[0][...] = jnp.where(row_odd, blocks[1], blocks[0])
    out_refs[1][...] = jnp.where(row_odd, blocks[0], blocks[1])
    out_refs[2][...] = jnp.where(col_odd, blocks[3], blocks[2])
    out_refs[3][...] = jnp.where(col_odd, blocks[2], blocks[3])


def extend(v, pieces):
    up, down, right, left = from_swaps(pieces)
    return jnp.concatenate([v, down, up, left, right], axis=0)


def picked_blocks(v, lists):
    got = gather_rows(v, lists)
    return [jnp.concatenate([got[d:d + 1], got[4 + d:5 + d]], axis=0) for d in range(4)]


def pick_kernel(v_ref, list_ref, point_ref, target_ref, same_ref, same_list_ref, *out_refs):
    same_ref[...] = v_ref[...]
    same_list_ref[...] = list_ref[...]
    put_outgoing(picked_blocks(v_ref[...], list_ref[...]), out_refs)
    lane = lax.broadcasted_iota(jnp.int32, (1, LANES), 1)
    own = jnp.zeros((1, LANES), F32)
    for c in range(3):
        part = point_ref[c:c + 1, 0:LANES]
        if c:
            part = pltpu.roll(part, TGT_DEV * c, 1)
        own = jnp.where((lane >= TGT_DEV * c) & (lane < TGT_DEV * (c + 1)), part, own)
    target_ref[...] = jnp.broadcast_to(own, (N_DEV, LANES))


def apply_kernel(live_ref, v_ref, ga, gb, gc, gd, conn_ref, grad_ref, vol_ref,
                 own_ref, oa, ob, oc, od, ext_ref, acc_ref, turn_ref):
    ext_ref[...] = extend(v_ref[...], [ga, gb, gc, gd])
    acc_ref[...] = jnp.zeros_like(acc_ref)

    def element_block(t, carry):
        grads, field = element_gradient(ext_ref[...], conn_ref, grad_ref, turn_ref, t)
        vol = block_volume(vol_ref, t)
        field = [vol * f for f in field]
        terms = [
            grads[3 * a] * field[0] + grads[3 * a + 1] * field[1] + grads[3 * a + 2] * field[2]
            for a in range(3)
        ]
        terms.append(-(terms[0] + terms[1] + terms[2]))
        total = acc_ref[...]
        for a in range(4):
            total = total + scatter_block(conn_block(conn_ref, a, t), terms[a], EXT_ROWS)
        acc_ref[...] = total
        return carry

    lax.fori_loop(0, live_ref[0], element_block, 0)
    own_ref[...] = acc_ref[0:OWN_ROWS, :]
    down, up, left, right = [
        acc_ref[OWN_ROWS + 2 * d:OWN_ROWS + 2 * d + 2, :] for d in range(4)
    ]
    put_outgoing([up, down, right, left], (oa, ob, oc, od))


def combine_kernel(own_ref, ra, rb, rc, rd, list_ref, v_ref, mass_ref,
                   next_ref, oa, ob, oc, od):
    lists = list_ref[...]
    back = from_swaps([ra, rb, rc, rd])
    terms = jnp.concatenate([b[0:1] for b in back] + [b[1:2] for b in back], axis=0)
    added = scatter_block(lists, terms, OWN_ROWS)
    value = (mass_ref[...] * v_ref[...] + own_ref[...] + added) * SCALE
    next_ref[...] = value
    put_outgoing(picked_blocks(value, lists), (oa, ob, oc, od))


def prepare_kernel(point_ref, cos_ref, angle_ref, area_ref, mass_ref, tgt_ref,
                   wide_ref, left_ref, right_ref, row_ref, same_mass_ref):
    same_mass_ref[...] = mass_ref[...]
    third = cos_ref[...].reshape(1, SLOTS)
    angle = angle_ref[...].reshape(1, SLOTS)
    area = area_ref[...].reshape(1, SLOTS) * inverse_four_pi
    sine = area * jnp.sqrt(1.0 - third * third)
    src = jnp.concatenate(
        [point_ref[...], sine * jnp.cos(angle), sine * jnp.sin(angle), area * third,
         jnp.zeros((2, SLOTS), F32)], axis=0,
    )
    src = jnp.concatenate([src, jnp.zeros((8, PAD_SLOTS - SLOTS), F32)], axis=1)
    cols = jnp.transpose(src)
    for c in range(6):
        wide_ref[c] = jnp.broadcast_to(cols[0:SLOTS, c:c + 1], (SLOTS, LANES))
    lane = lax.broadcasted_iota(jnp.int32, (TGT_ROWS, LANES), 1)
    for c in range(3):
        out = jnp.zeros((TGT_ROWS, LANES), F32)
        for j in range(4):
            part = tgt_ref[pl.ds(j, TGT_ROWS, stride=4), :]
            shift = (32 * j - 32 * c) % LANES
            if shift:
                part = pltpu.roll(part, shift, 1)
            out = jnp.where((lane >= 32 * j) & (lane < 32 * j + 32), part, out)
        row_ref[c] = out

    def factors(points, scale, extra, swap):
        norm = points[0] * points[0] + points[1] * points[1] + points[2] * points[2] + extra
        ones = jnp.ones_like(norm)
        lines = []
        for p in points:
            a = [q.astype(F32) for q in split_terms(p * scale)]
            order = (0, 1, 0, 1, 2, 0) if swap else (0, 0, 1, 1, 0, 2)
            lines += [a[k] for k in order]
        norms = [q.astype(F32) for q in split_terms(norm)]
        lines += [ones] * 3 + norms if swap else norms + [ones] * 3
        return lines

    left = factors([src[c:c + 1, :] - 0.5 for c in range(3)], 1.0, 0.0, False)
    left = jnp.concatenate(left + [jnp.zeros((KDIM - 24, PAD_SLOTS), F32)], axis=0)
    left_ref[...] = jnp.transpose(left)[0:SLOTS, :].astype(BF16)
    right = factors([row_ref[c] - 0.5 for c in range(3)], -2.0, smoothing, True)
    zero = jnp.zeros((1, LANES), F32)
    for g in range(TGT_ROWS):
        block = jnp.concatenate([r[g:g + 1, :] for r in right] + [zero] * (KDIM - 24), axis=0)
        right_ref[:, g * LANES:(g + 1) * LANES] = block.astype(BF16)


def entries_kernel(base, wide_ref, left_ref, right_ref, row_ref, entry_ref):
    def target_group(g, carry):
        first = base + g * GROUP
        lanes = pl.ds(pl.multiple_of(first * LANES, GROUP * LANES), GROUP * LANES)
        square = jnp.dot(left_ref[...], right_ref[:, lanes], preferred_element_type=F32)
        for s in range(SLOTS // 16):
            rows = slice(16 * s, 16 * s + 16)
            sx, sy, sz, wx, wy, wz = [wide_ref[c, rows, :] for c in range(6)]
            for q in range(GROUP):
                at = pl.ds(first + q, 1)
                inverse = lax.rsqrt(square[rows, q * LANES:(q + 1) * LANES])
                numerator = (
                    (row_ref[0, at, :] - sx) * wx
                    + (row_ref[1, at, :] - sy) * wy
                    + (row_ref[2, at, :] - sz) * wz
                )
                value = (numerator * (inverse * inverse * inverse)).astype(BF16)
                out = pl.ds(pl.multiple_of((g * GROUP + q) * LANES, LANES), LANES)
                entry_ref[rows, out] = value
        return carry

    lax.fori_loop(0, entry_ref.shape[1] // (GROUP * LANES), target_group, 0)


def far_kernel(live_ref, b_ref, v1_ref, v2_ref, ga, gb, gc, gd, conn_ref, grad_ref, vol_ref,
               mass_ref, node_ref, e0, e1, e2,
               out_ref, trace_ref, ext_ref, d0, d1, d2, lhs_ref, turn_ref):
    b = b_ref[...]
    v1 = v1_ref[...]
    v2 = v2_ref[...]
    ext_ref[...] = extend(v2, [ga, gb, gc, gd])

    def energy_block(t, total):
        _, field = element_gradient(ext_ref[...], conn_ref, grad_ref, turn_ref, t)
        return total + block_volume(vol_ref, t) * (
            field[0] * field[0] + field[1] * field[1] + field[2] * field[2]
        )

    energy = lax.fori_loop(0, live_ref[0], energy_block, jnp.zeros((8, LANES), F32))
    products = [b * b, b * v1, v1 * v1, v1 * v2, v2 * v2, mass_ref[...] * v2 * v2]
    sums = [p[0:8] + p[8:16] for p in products]
    sums[5] = (sums[5] + energy) * SCALE
    sub = lax.broadcasted_iota(jnp.int32, (8, LANES), 0)
    lane_row = lax.broadcasted_iota(jnp.int32, (1, LANES), 1)
    moments = jnp.zeros((1, LANES), F32)
    for k in range(6):
        moments = jnp.where(lane_row == 96 + k, jnp.sum(sums[k]), moments)

    nodes = node_ref[...]
    traces = [gather_rows(table, nodes) for table in (b, v1, v2)]
    for k in range(3):
        trace_ref[k] = traces[k]
    for r in range(PAD_SLOTS // LANES):
        block = jnp.zeros((8, LANES), F32)
        for k in range(3):
            t = traces[k][r:r + 1, :]
            high = t.astype(BF16).astype(F32)
            block = jnp.where(sub == 2 * k, high, block)
            block = jnp.where(sub == 2 * k + 1, t - high, block)
        lhs_ref[:, r * LANES:(r + 1) * LANES] = block.astype(BF16)
    lhs = lhs_ref[:, 0:SLOTS]
    base = 0
    for each, entry_ref in zip(CHUNKS, (e0, e1, e2)):
        res = jnp.dot(lhs, entry_ref[...], preferred_element_type=F32)
        base += each
        for q in range(each):
            at = slice(base - each + q, base - each + q + 1)
            part = res[:, q * LANES:(q + 1) * LANES]
            d0[at, :] = part[0:1] + part[1:2]
            d1[at, :] = part[2:3] + part[3:4]
            d2[at, :] = part[4:5] + part[5:6]

    lane = lax.broadcasted_iota(jnp.int32, (TGT_ROWS, LANES), 1)
    spread = jnp.broadcast_to(moments, (TGT_ROWS, LANES))
    for j in range(4):
        out = spread
        for k, ref in enumerate((d0, d1, d2)):
            part = ref[...]
            shift = (32 * k - 32 * j) % LANES
            if shift:
                part = pltpu.roll(part, shift, 1)
            out = jnp.where((lane >= 32 * k) & (lane < 32 * k + 32), part, out)
        out_ref[pl.ds(j, TGT_ROWS, stride=4), :] = out


def final_kernel(got_ref, b_ref, v1_ref, v2_ref, trace_ref, pot_ref, dir_ref):
    total = jnp.sum(got_ref[...], axis=0, keepdims=True)
    lane = lax.broadcasted_iota(jnp.int32, (1, LANES), 1)
    m = [jnp.sum(jnp.where(lane == 96 + k, total, 0.0), axis=1, keepdims=True) for k in range(6)]
    l1 = m[2] / m[1]
    l2 = m[3] / m[1]
    s11 = m[3] - l1 * m[2]
    s12 = m[4] - l1 * m[3]
    s22 = m[5] - l2 * m[3]
    y1 = m[1] - l1 * m[0]
    y2 = m[2] - l2 * m[0]
    keep1 = s11 > 4e-7 * m[3]
    safe11 = jnp.where(keep1, s11, 1.0)
    ratio = jnp.where(keep1, s12 / safe11, 0.0)
    d2 = s22 - ratio * s12
    keep2 = keep1 & (d2 > 4e-7 * m[5])
    c2 = jnp.where(keep2, (y2 - ratio * y1) / jnp.where(keep2, d2, 1.0), 0.0)
    c1 = jnp.where(keep1, (y1 - s12 * c2) / safe11, 0.0)
    c0 = (m[0] - m[2] * c1 - m[3] * c2) / m[1]
    c0 = c0 * SCALE
    c1 = c1 * SCALE
    c2 = c2 * SCALE
    pot_ref[...] = c0 * b_ref[...] + c1 * v1_ref[...] + c2 * v2_ref[...]
    out = jnp.zeros((1, LANES), F32)
    for k, c in enumerate((c0, c1, c2)):
        part = total
        if k:
            part = pltpu.roll(total, LANES - 32 * k, 1)
        out = out + c * (part - 0.5 * trace_ref[k, 0:1, :])
    dir_ref[...] = out[:, 0:TGT_DEV]


def call(body, out_shapes, args, smem=0, scratch=(), cost=2000000):
    specs = [pl.BlockSpec(memory_space=pltpu.SMEM)] * smem
    specs += [pl.BlockSpec(memory_space=pltpu.VMEM)] * (len(args) - smem)
    out_shapes = [o if isinstance(o, jax.ShapeDtypeStruct) else jax.ShapeDtypeStruct(o, F32) for o in out_shapes]
    return pl.pallas_call(
        body,
        out_shape=out_shapes,
        in_specs=specs,
        out_specs=[pl.BlockSpec(memory_space=pltpu.VMEM)] * len(out_shapes),
        scratch_shapes=list(scratch),
        compiler_params=pltpu.CompilerParams(vmem_limit_bytes=VMEM_GRANT),
        cost_estimate=pl.CostEstimate(flops=cost, bytes_accessed=1 << 20, transcendentals=0),
    )(*args)


PIECE = (2, LANES)
TURN = pltpu.VMEM((72, LANES), F32)


def swap_partners(rows, cols, axis, second):
    out = []
    for r in range(rows):
        for c in range(cols):
            me, count = (r, rows) if axis == "row" else (c, cols)
            if not second:
                other = me ^ 1
            elif 0 < me < count - 1:
                other = ((me + 1) ^ 1) - 1
            else:
                other = None
            if axis == "row":
                pair = (other, c) if other is not None else (r, c ^ 1)
            else:
                pair = (r, other) if other is not None else (r ^ 1, c)
            out.append((r * cols + c, pair[0] * cols + pair[1]))
    return out


def exchange(pieces):
    rows = lax.axis_size("row")
    cols = lax.axis_size("col")
    got = []
    for k in range(4):
        axis = "row" if k < 2 else "col"
        got.append(lax.ppermute(pieces[k], ("row", "col"), swap_partners(rows, cols, axis, k % 2 == 1)))
    return got


def per_device(connectivity, gradients, volumes, live_blocks, send_lists, divergence, mass_shift,
               boundary_nodes, surface_points, normal_cos, normal_angle, node_areas):
    conn = connectivity.reshape(4, ELEM_ROWS, LANES).transpose(1, 0, 2).reshape(4 * ELEM_ROWS, LANES)
    vol = volumes.reshape(ELEM_ROWS, LANES)
    lists = send_lists.reshape(4, 2, LANES).transpose(1, 0, 2).reshape(8, LANES)
    b = divergence.reshape(OWN_ROWS, LANES)
    mass = mass_shift.reshape(OWN_ROWS, LANES)
    nodes = jnp.pad(boundary_nodes, (0, 8 * LANES - SLOTS)).reshape(8, LANES)
    elements = (conn, gradients, vol)

    mine, b, lists, *pieces = call(
        pick_kernel,
        [(N_DEV, LANES), b.shape, jax.ShapeDtypeStruct(lists.shape, lists.dtype)] + [PIECE] * 4,
        (b, lists, surface_points),
    )
    targets = lax.all_to_all(mine, ("row", "col"), 0, 0, tiled=True)
    prepared = None
    chunks = []

    def fill():
        nonlocal prepared, mass
        if prepared is None:
            prepared = call(
                prepare_kernel,
                [
                    (6, SLOTS, LANES),
                    jax.ShapeDtypeStruct((SLOTS, KDIM), BF16),
                    jax.ShapeDtypeStruct((KDIM, TGT_ROWS * LANES), BF16),
                    (3, TGT_ROWS, LANES),
                    mass.shape,
                ],
                (surface_points, normal_cos, normal_angle, node_areas, mass, targets),
            )
            *prepared, mass = prepared
            return
        done = len(chunks)
        base = sum(CHUNKS[:done])
        chunks.append(call(
            lambda *refs: entries_kernel(base, *refs),
            [jax.ShapeDtypeStruct((SLOTS, CHUNKS[done] * LANES), BF16)],
            prepared,
        )[0])

    def swap(number, pieces):
        out = exchange(pieces)
        if number:
            fill()
        return out

    vectors = [b]
    for step in range(2):
        ghosts = swap(2 * step, pieces)
        own, *back = call(
            apply_kernel, [(OWN_ROWS, LANES)] + [PIECE] * 4,
            (live_blocks, vectors[-1], *ghosts, *elements), smem=1,
            scratch=[pltpu.VMEM((EXT_ROWS, LANES), F32), pltpu.VMEM((HIGH_ROWS, LANES), F32), TURN],
        )
        returned = swap(2 * step + 1, back)
        new, *pieces = call(
            combine_kernel, [(OWN_ROWS, LANES)] + [PIECE] * 4,
            (own, *returned, lists, vectors[-1], mass),
        )
        vectors.append(new)
    ghosts = swap(4, pieces)
    partial, trace = call(
        far_kernel, [(N_DEV, LANES), (3, 8, LANES)],
        (live_blocks, *vectors, *ghosts, *elements, mass, nodes, *chunks), smem=1,
        scratch=[pltpu.VMEM((EXT_ROWS, LANES), F32)]
        + [pltpu.VMEM((TGT_ROWS, LANES), F32)] * 3
        + [pltpu.VMEM((8, PAD_SLOTS), BF16), TURN],
    )
    got = lax.all_to_all(partial, ("row", "col"), 0, 0, tiled=True)
    potential, dirichlet = call(
        final_kernel, [(OWN_ROWS, LANES), (1, TGT_DEV)], (got, *vectors, trace)
    )
    return potential.reshape(NN_DEV), dirichlet.reshape(TGT_DEV)


def solution(mesh):
    both = ("row", "col")

    return jax.shard_map(
        per_device,
        mesh=mesh,
        in_specs=(
            P(None, both), P(None, both), P(both), P(both), P(None, both), P(both),
            P(both), P(both), P(None, both), P(both), P(both), P(both),
        ),
        out_specs=(P(both), P(both)),
        check_vma=False,
    )
```

```python
import math

import jax
import jax.numpy as jnp
from jax import lax
from jax.experimental import pallas as pl
from jax.experimental.pallas import tpu as pltpu
from jax.sharding import PartitionSpec as P


F32 = jnp.float32
BF16 = jnp.bfloat16
LANES = 128
NN_DEV = 2048
EBLK = 1024
GH = 256
TGT_DEV = 32
OWN_ROWS = NN_DEV // LANES
EXT_ROWS = OWN_ROWS + 4 * GH // LANES
HIGH_ROWS = 32
SLOTS = 320
PAD_SLOTS = 384
N_DEV = 256
TGT_ROWS = N_DEV // 4
CHUNKS = (20, 24, 20)
GROUP = 4
KDIM = 32
SPLITS = 3
SCALE = 1.0 / 64.0
B_ROWS = slice(0, 16)
MASS_ROWS = slice(16, 32)
COS_ROWS = slice(32, 35)
ANGLE_ROWS = slice(35, 38)
AREA_ROWS = slice(38, 41)
VMEM_GRANT = 16 << 20
smoothing = 0.0001
inverse_four_pi = 1.0 / (4.0 * math.pi)


def gather_rows(table, index):
    high = index >> 7
    low = index & 127
    out = jnp.zeros(index.shape, F32)
    for r in range(table.shape[0]):
        row = jnp.broadcast_to(table[r:r + 1, :], index.shape)
        out = jnp.where(high == r, jnp.take_along_axis(row, low, axis=1), out)
    return out


def split_terms(terms, count=SPLITS):
    parts = []
    for _ in range(count):
        parts.append(terms.astype(BF16))
        terms = terms - parts[-1].astype(F32)
    return parts


def scatter_block(index, terms, rows):
    rows = -(-rows // 16) * 16
    sub = lax.broadcasted_iota(jnp.int32, (LANES, LANES), 0).astype(F32).astype(BF16)
    sub_rows = lax.broadcasted_iota(jnp.int32, (rows, LANES), 0).astype(F32).astype(BF16)
    one = jnp.ones((LANES, LANES), BF16)
    zero = jnp.zeros((LANES, LANES), BF16)
    zero_rows = jnp.zeros((rows, LANES), BF16)
    low = (index & 127).astype(F32)
    high = (index >> 7).astype(F32)
    parts = [p.astype(F32) for p in split_terms(terms)]
    hot_blocks = []
    weight_blocks = []
    for s in range(8):
        at = slice(s, s + 1)
        low_row = jnp.broadcast_to(low[at], (LANES, LANES)).astype(BF16)
        hot_blocks.append(jnp.where(sub == low_row, one, zero))
        mine = sub_rows == jnp.broadcast_to(high[at], (rows, LANES)).astype(BF16)
        weight_blocks.append(jnp.concatenate(
            [jnp.where(mine, jnp.broadcast_to(p[at], (rows, LANES)).astype(BF16), zero_rows) for p in parts],
            axis=0,
        ))
    total = lax.dot_general(
        jnp.concatenate(weight_blocks, axis=1), jnp.concatenate(hot_blocks, axis=1),
        (((1,), (1,)), ((), ())), preferred_element_type=F32,
    )
    out = total[0:rows]
    for k in range(1, SPLITS):
        out = out + total[k * rows:(k + 1) * rows]
    return out


def turn_block(data_ref, turn_ref, t):
    for k in range(8):
        lanes = pl.ds(pl.multiple_of(EBLK * t + LANES * k, LANES), LANES)
        turn_ref[16 * k:16 * k + 8, :] = data_ref[0:8, lanes]
        turn_ref[16 * k + 8:16 * k + 14, :] = data_ref[8:14, lanes]
    rows = [turn_ref[pl.ds(q, 8, stride=16), :] for q in range(14)]
    return rows[0:9], [r.astype(jnp.int32) for r in rows[9:13]], rows[13]


def element_gradient(ext, data_ref, turn_ref, t):
    grads, index, volume = turn_block(data_ref, turn_ref, t)
    corner = [gather_rows(ext, i) for i in index]
    diff = [corner[a] - corner[3] for a in range(3)]
    field = [
        grads[k] * diff[0] + grads[3 + k] * diff[1] + grads[6 + k] * diff[2]
        for k in range(3)
    ]
    return grads, index, volume, field


def odd(axis):
    return lax.rem(lax.axis_index(axis), 2) == 1


def inside(axis):
    me = lax.axis_index(axis)
    return (me > 0) & (me < lax.axis_size(axis) - 1)


def from_swaps(pieces):
    row_a, row_b, col_a, col_b = [p[...] for p in pieces]
    row_b = jnp.where(inside("row"), row_b, 0.0)
    col_b = jnp.where(inside("col"), col_b, 0.0)
    row_odd = odd("row")
    col_odd = odd("col")
    return [
        jnp.where(row_odd, row_b, row_a),
        jnp.where(row_odd, row_a, row_b),
        jnp.where(col_odd, col_b, col_a),
        jnp.where(col_odd, col_a, col_b),
    ]


def put_outgoing(blocks, out_refs):
    row_odd = odd("row")
    col_odd = odd("col")
    out_refs[0][...] = jnp.where(row_odd, blocks[1], blocks[0])
    out_refs[1][...] = jnp.where(row_odd, blocks[0], blocks[1])
    out_refs[2][...] = jnp.where(col_odd, blocks[3], blocks[2])
    out_refs[3][...] = jnp.where(col_odd, blocks[2], blocks[3])


def extend(v, pieces):
    up, down, right, left = from_swaps(pieces)
    return jnp.concatenate([v, down, up, left, right], axis=0)


def picked_blocks(v, lists):
    got = gather_rows(v, lists)
    return [jnp.concatenate([got[d:d + 1], got[4 + d:5 + d]], axis=0) for d in range(4)]


def pick_kernel(small_ref, list_ref, point_ref, target_ref, same_list_ref, same_point_ref, *out_refs):
    same_list_ref[...] = list_ref[...]
    same_point_ref[...] = point_ref[...]
    put_outgoing(picked_blocks(small_ref[B_ROWS, :], list_ref[...]), out_refs)
    lane = lax.broadcasted_iota(jnp.int32, (1, LANES), 1)
    own = jnp.zeros((1, LANES), F32)
    for c in range(3):
        part = point_ref[c:c + 1, 0:LANES]
        if c:
            part = pltpu.roll(part, TGT_DEV * c, 1)
        own = jnp.where((lane >= TGT_DEV * c) & (lane < TGT_DEV * (c + 1)), part, own)
    target_ref[...] = jnp.broadcast_to(own, (N_DEV, LANES))


def apply_kernel(live_ref, v_ref, ga, gb, gc, gd, data_ref,
                 own_ref, oa, ob, oc, od, ext_ref, acc_ref, turn_ref):
    ext_ref[...] = extend(v_ref[0:OWN_ROWS, :], [ga, gb, gc, gd])
    acc_ref[...] = jnp.zeros_like(acc_ref)

    def element_block(t, carry):
        grads, index, volume, field = element_gradient(ext_ref[...], data_ref, turn_ref, t)
        field = [volume * f for f in field]
        terms = [
            grads[3 * a] * field[0] + grads[3 * a + 1] * field[1] + grads[3 * a + 2] * field[2]
            for a in range(3)
        ]
        terms.append(-(terms[0] + terms[1] + terms[2]))
        total = acc_ref[...]
        for a in range(4):
            total = total + scatter_block(index[a], terms[a], EXT_ROWS)
        acc_ref[...] = total
        return carry

    lax.fori_loop(0, live_ref[0], element_block, 0)
    own_ref[...] = acc_ref[0:OWN_ROWS, :]
    down, up, left, right = [
        acc_ref[OWN_ROWS + 2 * d:OWN_ROWS + 2 * d + 2, :] for d in range(4)
    ]
    put_outgoing([up, down, right, left], (oa, ob, oc, od))


def combine_kernel(own_ref, ra, rb, rc, rd, list_ref, v_ref, small_ref,
                   next_ref, oa, ob, oc, od):
    lists = list_ref[...]
    back = from_swaps([ra, rb, rc, rd])
    terms = jnp.concatenate([b[0:1] for b in back] + [b[1:2] for b in back], axis=0)
    added = scatter_block(lists, terms, OWN_ROWS)
    value = (small_ref[MASS_ROWS, :] * v_ref[0:OWN_ROWS, :] + own_ref[...] + added) * SCALE
    next_ref[...] = value
    put_outgoing(picked_blocks(value, lists), (oa, ob, oc, od))


def prepare_kernel(small_ref, point_ref, tgt_ref, wide_ref, left_ref, right_ref, row_ref):
    def line(rows):
        return jnp.concatenate([small_ref[r:r + 1, :] for r in range(rows.start, rows.stop)], axis=1)

    third = line(COS_ROWS)
    angle = line(ANGLE_ROWS)
    area = line(AREA_ROWS) * inverse_four_pi
    sine = area * jnp.sqrt(1.0 - third * third)
    points = jnp.concatenate([point_ref[...], jnp.zeros((3, PAD_SLOTS - SLOTS), F32)], axis=1)
    src = jnp.concatenate(
        [points, sine * jnp.cos(angle), sine * jnp.sin(angle), area * third, jnp.zeros((2, PAD_SLOTS), F32)],
        axis=0,
    )
    cols = jnp.transpose(src)
    for c in range(6):
        wide_ref[c] = jnp.broadcast_to(cols[0:SLOTS, c:c + 1], (SLOTS, LANES))
    lane = lax.broadcasted_iota(jnp.int32, (TGT_ROWS, LANES), 1)
    for c in range(3):
        out = jnp.zeros((TGT_ROWS, LANES), F32)
        for j in range(4):
            part = tgt_ref[pl.ds(j, TGT_ROWS, stride=4), :]
            shift = (32 * j - 32 * c) % LANES
            if shift:
                part = pltpu.roll(part, shift, 1)
            out = jnp.where((lane >= 32 * j) & (lane < 32 * j + 32), part, out)
        row_ref[c] = out

    def factors(points, scale, extra, swap):
        norm = points[0] * points[0] + points[1] * points[1] + points[2] * points[2] + extra
        ones = jnp.ones_like(norm)
        lines = []
        for p in points:
            a = [q.astype(F32) for q in split_terms(p * scale)]
            order = (0, 1, 0, 1, 2, 0) if swap else (0, 0, 1, 1, 0, 2)
            lines += [a[k] for k in order]
        norms = [q.astype(F32) for q in split_terms(norm)]
        lines += [ones] * 3 + norms if swap else norms + [ones] * 3
        return lines

    left = factors([src[c:c + 1, :] - 0.5 for c in range(3)], 1.0, 0.0, False)
    left = jnp.concatenate(left + [jnp.zeros((KDIM - 24, PAD_SLOTS), F32)], axis=0)
    left_ref[...] = jnp.transpose(left)[0:SLOTS, :].astype(BF16)
    right = factors([row_ref[c] - 0.5 for c in range(3)], -2.0, smoothing, True)
    zero = jnp.zeros((1, LANES), F32)
    for g in range(TGT_ROWS):
        block = jnp.concatenate([r[g:g + 1, :] for r in right] + [zero] * (KDIM - 24), axis=0)
        right_ref[:, g * LANES:(g + 1) * LANES] = block.astype(BF16)


def entries_kernel(base, wide_ref, left_ref, right_ref, row_ref, entry_ref):
    def target_group(g, carry):
        first = base + g * GROUP
        lanes = pl.ds(pl.multiple_of(first * LANES, GROUP * LANES), GROUP * LANES)
        square = jnp.dot(left_ref[...], right_ref[:, lanes], preferred_element_type=F32)
        for s in range(SLOTS // 16):
            rows = slice(16 * s, 16 * s + 16)
            sx, sy, sz, wx, wy, wz = [wide_ref[c, rows, :] for c in range(6)]
            for q in range(GROUP):
                at = pl.ds(first + q, 1)
                inverse = lax.rsqrt(square[rows, q * LANES:(q + 1) * LANES])
                numerator = (
                    (row_ref[0, at, :] - sx) * wx
                    + (row_ref[1, at, :] - sy) * wy
                    + (row_ref[2, at, :] - sz) * wz
                )
                value = (numerator * (inverse * inverse * inverse)).astype(BF16)
                out = pl.ds(pl.multiple_of((g * GROUP + q) * LANES, LANES), LANES)
                entry_ref[rows, out] = value
        return carry

    lax.fori_loop(0, entry_ref.shape[1] // (GROUP * LANES), target_group, 0)


def far_kernel(live_ref, small_ref, v1_ref, v2_ref, ga, gb, gc, gd, data_ref, node_ref, e0, e1, e2,
               out_ref, trace_ref, ext_ref, d0, d1, d2, lhs_ref, turn_ref):
    b = small_ref[B_ROWS, :]
    v1 = v1_ref[...]
    v2 = v2_ref[...]
    ext_ref[...] = extend(v2, [ga, gb, gc, gd])

    def energy_block(t, total):
        _, _, volume, field = element_gradient(ext_ref[...], data_ref, turn_ref, t)
        return total + volume * (
            field[0] * field[0] + field[1] * field[1] + field[2] * field[2]
        )

    energy = lax.fori_loop(0, live_ref[0], energy_block, jnp.zeros((8, LANES), F32))
    products = [b * b, b * v1, v1 * v1, v1 * v2, v2 * v2, small_ref[MASS_ROWS, :] * v2 * v2]
    sums = [p[0:8] + p[8:16] for p in products]
    sums[5] = (sums[5] + energy) * SCALE
    sub = lax.broadcasted_iota(jnp.int32, (8, LANES), 0)
    lane_row = lax.broadcasted_iota(jnp.int32, (1, LANES), 1)
    moments = jnp.zeros((1, LANES), F32)
    for k in range(6):
        moments = jnp.where(lane_row == 96 + k, jnp.sum(sums[k]), moments)

    nodes = node_ref[...]
    traces = [gather_rows(table, nodes) for table in (b, v1, v2)]
    for k in range(3):
        trace_ref[k] = traces[k]
    for r in range(PAD_SLOTS // LANES):
        block = jnp.zeros((8, LANES), F32)
        for k in range(3):
            t = traces[k][r:r + 1, :]
            high = t.astype(BF16).astype(F32)
            block = jnp.where(sub == 2 * k, high, block)
            block = jnp.where(sub == 2 * k + 1, t - high, block)
        lhs_ref[:, r * LANES:(r + 1) * LANES] = block.astype(BF16)
    lhs = lhs_ref[:, 0:SLOTS]
    base = 0
    for each, entry_ref in zip(CHUNKS, (e0, e1, e2)):
        res = jnp.dot(lhs, entry_ref[...], preferred_element_type=F32)
        base += each
        for q in range(each):
            at = slice(base - each + q, base - each + q + 1)
            part = res[:, q * LANES:(q + 1) * LANES]
            d0[at, :] = part[0:1] + part[1:2]
            d1[at, :] = part[2:3] + part[3:4]
            d2[at, :] = part[4:5] + part[5:6]

    lane = lax.broadcasted_iota(jnp.int32, (TGT_ROWS, LANES), 1)
    spread = jnp.broadcast_to(moments, (TGT_ROWS, LANES))
    for j in range(4):
        out = spread
        for k, ref in enumerate((d0, d1, d2)):
            part = ref[...]
            shift = (32 * k - 32 * j) % LANES
            if shift:
                part = pltpu.roll(part, shift, 1)
            out = jnp.where((lane >= 32 * k) & (lane < 32 * k + 32), part, out)
        out_ref[pl.ds(j, TGT_ROWS, stride=4), :] = out


def final_kernel(got_ref, small_ref, v1_ref, v2_ref, trace_ref, pot_ref, dir_ref):
    total = jnp.sum(got_ref[...], axis=0, keepdims=True)
    lane = lax.broadcasted_iota(jnp.int32, (1, LANES), 1)
    m = [jnp.sum(jnp.where(lane == 96 + k, total, 0.0), axis=1, keepdims=True) for k in range(6)]
    l1 = m[2] / m[1]
    l2 = m[3] / m[1]
    s11 = m[3] - l1 * m[2]
    s12 = m[4] - l1 * m[3]
    s22 = m[5] - l2 * m[3]
    y1 = m[1] - l1 * m[0]
    y2 = m[2] - l2 * m[0]
    keep1 = s11 > 4e-7 * m[3]
    safe11 = jnp.where(keep1, s11, 1.0)
    ratio = jnp.where(keep1, s12 / safe11, 0.0)
    d2 = s22 - ratio * s12
    keep2 = keep1 & (d2 > 4e-7 * m[5])
    c2 = jnp.where(keep2, (y2 - ratio * y1) / jnp.where(keep2, d2, 1.0), 0.0)
    c1 = jnp.where(keep1, (y1 - s12 * c2) / safe11, 0.0)
    c0 = (m[0] - m[2] * c1 - m[3] * c2) / m[1]
    c0 = c0 * SCALE
    c1 = c1 * SCALE
    c2 = c2 * SCALE
    pot_ref[...] = c0 * small_ref[B_ROWS, :] + c1 * v1_ref[...] + c2 * v2_ref[...]
    out = jnp.zeros((1, LANES), F32)
    for k, c in enumerate((c0, c1, c2)):
        part = total
        if k:
            part = pltpu.roll(total, LANES - 32 * k, 1)
        out = out + c * (part - 0.5 * trace_ref[k, 0:1, :])
    dir_ref[...] = out[:, 0:TGT_DEV]


def call(body, out_shapes, args, smem=0, scratch=(), cost=2000000):
    specs = [pl.BlockSpec(memory_space=pltpu.SMEM)] * smem
    specs += [pl.BlockSpec(memory_space=pltpu.VMEM)] * (len(args) - smem)
    out_shapes = [o if isinstance(o, jax.ShapeDtypeStruct) else jax.ShapeDtypeStruct(o, F32) for o in out_shapes]
    return pl.pallas_call(
        body,
        out_shape=out_shapes,
        in_specs=specs,
        out_specs=[pl.BlockSpec(memory_space=pltpu.VMEM)] * len(out_shapes),
        scratch_shapes=list(scratch),
        compiler_params=pltpu.CompilerParams(vmem_limit_bytes=VMEM_GRANT),
        cost_estimate=pl.CostEstimate(flops=cost, bytes_accessed=1 << 20, transcendentals=0),
    )(*args)


PIECE = (2, LANES)
TURN = pltpu.VMEM((128, LANES), F32)


def swap_partners(rows, cols, axis, second):
    out = []
    for r in range(rows):
        for c in range(cols):
            me, count = (r, rows) if axis == "row" else (c, cols)
            if not second:
                other = me ^ 1
            elif 0 < me < count - 1:
                other = ((me + 1) ^ 1) - 1
            else:
                other = None
            if axis == "row":
                pair = (other, c) if other is not None else (r, c ^ 1)
            else:
                pair = (r, other) if other is not None else (r ^ 1, c)
            out.append((r * cols + c, pair[0] * cols + pair[1]))
    return out


def exchange(pieces):
    rows = lax.axis_size("row")
    cols = lax.axis_size("col")
    got = []
    for k in range(4):
        axis = "row" if k < 2 else "col"
        got.append(lax.ppermute(pieces[k], ("row", "col"), swap_partners(rows, cols, axis, k % 2 == 1)))
    return got


def per_device(connectivity, gradients, volumes, live_blocks, send_lists, divergence, mass_shift,
               boundary_nodes, surface_points, normal_cos, normal_angle, node_areas):
    lists = send_lists.reshape(4, 2, LANES).transpose(1, 0, 2).reshape(8, LANES)
    nodes = jnp.pad(boundary_nodes, (0, 8 * LANES - SLOTS)).reshape(8, LANES)
    gap = jnp.zeros(PAD_SLOTS - SLOTS, F32)
    small = jnp.concatenate([
        divergence, mass_shift, normal_cos, gap, normal_angle, gap, node_areas, gap,
    ]).reshape(-1, LANES)
    data = jnp.concatenate([gradients, connectivity.astype(F32), volumes[None]], axis=0)
    mine, lists, points, *pieces = call(
        pick_kernel,
        [(N_DEV, LANES), jax.ShapeDtypeStruct(lists.shape, lists.dtype), surface_points.shape] + [PIECE] * 4,
        (small, lists, surface_points),
    )
    targets = lax.all_to_all(mine, ("row", "col"), 0, 0, tiled=True)
    prepared = None
    chunks = []

    def fill():
        nonlocal prepared
        if prepared is None:
            prepared = call(
                prepare_kernel,
                [
                    (6, SLOTS, LANES),
                    jax.ShapeDtypeStruct((SLOTS, KDIM), BF16),
                    jax.ShapeDtypeStruct((KDIM, TGT_ROWS * LANES), BF16),
                    (3, TGT_ROWS, LANES),
                ],
                (small, points, targets),
            )
            return
        done = len(chunks)
        base = sum(CHUNKS[:done])
        chunks.append(call(
            lambda *refs: entries_kernel(base, *refs),
            [jax.ShapeDtypeStruct((SLOTS, CHUNKS[done] * LANES), BF16)],
            prepared,
        )[0])

    def swap(number, pieces):
        out = exchange(pieces)
        if number:
            fill()
        return out

    vectors = [small]
    for step in range(2):
        ghosts = swap(2 * step, pieces)
        own, *back = call(
            apply_kernel, [(OWN_ROWS, LANES)] + [PIECE] * 4,
            (live_blocks, vectors[-1], *ghosts, data), smem=1,
            scratch=[pltpu.VMEM((EXT_ROWS, LANES), F32), pltpu.VMEM((HIGH_ROWS, LANES), F32), TURN],
        )
        returned = swap(2 * step + 1, back)
        new, *pieces = call(
            combine_kernel, [(OWN_ROWS, LANES)] + [PIECE] * 4,
            (own, *returned, lists, vectors[-1], small),
        )
        vectors.append(new)
    ghosts = swap(4, pieces)
    partial, trace = call(
        far_kernel, [(N_DEV, LANES), (3, 8, LANES)],
        (live_blocks, *vectors, *ghosts, data, nodes, *chunks), smem=1,
        scratch=[pltpu.VMEM((EXT_ROWS, LANES), F32)]
        + [pltpu.VMEM((TGT_ROWS, LANES), F32)] * 3
        + [pltpu.VMEM((8, PAD_SLOTS), BF16), TURN],
    )
    got = lax.all_to_all(partial, ("row", "col"), 0, 0, tiled=True)
    potential, dirichlet = call(
        final_kernel, [(OWN_ROWS, LANES), (1, TGT_DEV)], (got, *vectors, trace)
    )
    return potential.reshape(NN_DEV), dirichlet.reshape(TGT_DEV)


def solution(mesh):
    both = ("row", "col")

    return jax.shard_map(
        per_device,
        mesh=mesh,
        in_specs=(
            P(None, both), P(None, both), P(both), P(both), P(None, both), P(both),
            P(both), P(both), P(None, both), P(both), P(both), P(both),
        ),
        out_specs=(P(both), P(both)),
        check_vma=False,
    )
```

```python
import math

import jax
import jax.numpy as jnp
from jax import lax
from jax.experimental import pallas as pl
from jax.experimental.pallas import tpu as pltpu
from jax.sharding import PartitionSpec as P


F32 = jnp.float32
BF16 = jnp.bfloat16
LANES = 128
NN_DEV = 2048
EBLK = 1024
BLOCKS = 8
GH = 256
TGT_DEV = 32
OWN_ROWS = NN_DEV // LANES
EXT_ROWS = OWN_ROWS + 4 * GH // LANES
HIGH_ROWS = 32
SLOTS = 320
PAD_SLOTS = 384
N_DEV = 256
TGT_ROWS = N_DEV // 4
CHUNKS = (20, 24, 20)
GROUP = 4
KDIM = 32
SPLITS = 2
SCALE = 1.0 / 64.0
B_ROWS = slice(0, 16)
MASS_ROWS = slice(16, 32)
COS_ROWS = slice(32, 35)
ANGLE_ROWS = slice(35, 38)
AREA_ROWS = slice(38, 41)
VMEM_GRANT = 16 << 20
smoothing = 0.0001
inverse_four_pi = 1.0 / (4.0 * math.pi)


def gather_rows(table, index):
    high = index >> 7
    low = index & 127
    out = jnp.zeros(index.shape, F32)
    for r in range(table.shape[0]):
        row = jnp.broadcast_to(table[r:r + 1, :], index.shape)
        out = jnp.where(high == r, jnp.take_along_axis(row, low, axis=1), out)
    return out


def split_terms(terms, count):
    parts = []
    for _ in range(count):
        parts.append(terms.astype(BF16))
        terms = terms - parts[-1].astype(F32)
    return parts


def scatter_block(index, terms, rows):
    rows = -(-rows // 16) * 16
    sub = lax.broadcasted_iota(jnp.int32, (LANES, LANES), 0).astype(F32).astype(BF16)
    sub_rows = lax.broadcasted_iota(jnp.int32, (rows, LANES), 0).astype(F32).astype(BF16)
    one = jnp.ones((LANES, LANES), BF16)
    zero = jnp.zeros((LANES, LANES), BF16)
    zero_rows = jnp.zeros((rows, LANES), BF16)
    low = (index & 127).astype(F32)
    high = (index >> 7).astype(F32)
    parts = [p.astype(F32) for p in split_terms(terms, SPLITS)]
    hot_blocks = []
    weight_blocks = []
    for s in range(8):
        at = slice(s, s + 1)
        low_row = jnp.broadcast_to(low[at], (LANES, LANES)).astype(BF16)
        hot_blocks.append(jnp.where(sub == low_row, one, zero))
        mine = sub_rows == jnp.broadcast_to(high[at], (rows, LANES)).astype(BF16)
        weight_blocks.append(jnp.concatenate(
            [jnp.where(mine, jnp.broadcast_to(p[at], (rows, LANES)).astype(BF16), zero_rows) for p in parts],
            axis=0,
        ))
    total = lax.dot_general(
        jnp.concatenate(weight_blocks, axis=1), jnp.concatenate(hot_blocks, axis=1),
        (((1,), (1,)), ((), ())), preferred_element_type=F32,
    )
    out = total[0:rows]
    for k in range(1, SPLITS):
        out = out + total[k * rows:(k + 1) * rows]
    return out


def turn_block(data_ref, turn_ref, t):
    for k in range(8):
        lanes = pl.ds(pl.multiple_of(EBLK * t + LANES * k, LANES), LANES)
        turn_ref[16 * k:16 * k + 8, :] = data_ref[0:8, lanes]
        turn_ref[16 * k + 8:16 * k + 14, :] = data_ref[8:14, lanes]
    rows = [turn_ref[pl.ds(q, 8, stride=16), :] for q in range(14)]
    return rows[0:9], [r.astype(jnp.int32) for r in rows[9:13]], rows[13]


def element_gradient(ext, data_ref, turn_ref, t):
    grads, index, volume = turn_block(data_ref, turn_ref, t)
    corner = [gather_rows(ext, i) for i in index]
    diff = [corner[a] - corner[3] for a in range(3)]
    field = [
        grads[k] * diff[0] + grads[3 + k] * diff[1] + grads[6 + k] * diff[2]
        for k in range(3)
    ]
    return grads, index, volume, field


def odd(axis):
    return lax.rem(lax.axis_index(axis), 2) == 1


def inside(axis):
    me = lax.axis_index(axis)
    return (me > 0) & (me < lax.axis_size(axis) - 1)


def from_swaps(pieces):
    row_a, row_b, col_a, col_b = [p[...] for p in pieces]
    row_b = jnp.where(inside("row"), row_b, 0.0)
    col_b = jnp.where(inside("col"), col_b, 0.0)
    row_odd = odd("row")
    col_odd = odd("col")
    return [
        jnp.where(row_odd, row_b, row_a),
        jnp.where(row_odd, row_a, row_b),
        jnp.where(col_odd, col_b, col_a),
        jnp.where(col_odd, col_a, col_b),
    ]


def put_outgoing(blocks, out_refs):
    row_odd = odd("row")
    col_odd = odd("col")
    out_refs[0][...] = jnp.where(row_odd, blocks[1], blocks[0])
    out_refs[1][...] = jnp.where(row_odd, blocks[0], blocks[1])
    out_refs[2][...] = jnp.where(col_odd, blocks[3], blocks[2])
    out_refs[3][...] = jnp.where(col_odd, blocks[2], blocks[3])


def extend(v, pieces):
    up, down, right, left = from_swaps(pieces)
    return jnp.concatenate([v, down, up, left, right], axis=0)


def picked_blocks(v, lists):
    got = gather_rows(v, lists)
    return [jnp.concatenate([got[d:d + 1], got[4 + d:5 + d]], axis=0) for d in range(4)]


def pick_kernel(small_ref, list_ref, point_ref, target_ref, same_list_ref, same_point_ref, *out_refs):
    same_list_ref[...] = list_ref[...]
    same_point_ref[...] = point_ref[...]
    put_outgoing(picked_blocks(small_ref[B_ROWS, :], list_ref[...]), out_refs)
    lane = lax.broadcasted_iota(jnp.int32, (1, LANES), 1)
    own = jnp.zeros((1, LANES), F32)
    for c in range(3):
        part = point_ref[c:c + 1, 0:LANES]
        if c:
            part = pltpu.roll(part, TGT_DEV * c, 1)
        own = jnp.where((lane >= TGT_DEV * c) & (lane < TGT_DEV * (c + 1)), part, own)
    target_ref[...] = jnp.broadcast_to(own, (N_DEV, LANES))


def apply_kernel(live_ref, v_ref, ga, gb, gc, gd, data_ref,
                 own_ref, oa, ob, oc, od, ext_ref, acc_ref, turn_ref):
    ext_ref[...] = extend(v_ref[0:OWN_ROWS, :], [ga, gb, gc, gd])
    acc_ref[...] = jnp.zeros_like(acc_ref)

    def element_terms(t):
        grads, index, volume, field = element_gradient(
            ext_ref[...], data_ref, turn_ref, jnp.minimum(t, BLOCKS - 1)
        )
        field = [volume * f for f in field]
        terms = [
            grads[3 * a] * field[0] + grads[3 * a + 1] * field[1] + grads[3 * a + 2] * field[2]
            for a in range(3)
        ]
        terms.append(-(terms[0] + terms[1] + terms[2]))
        return tuple(index), tuple(terms)

    def element_block(t, carry):
        index, terms = carry
        following = element_terms(t + 1)
        total = acc_ref[...]
        for a in range(4):
            total = total + scatter_block(index[a], terms[a], EXT_ROWS)
        acc_ref[...] = total
        return following

    lax.fori_loop(0, live_ref[0], element_block, element_terms(0))
    own_ref[...] = acc_ref[0:OWN_ROWS, :]
    down, up, left, right = [
        acc_ref[OWN_ROWS + 2 * d:OWN_ROWS + 2 * d + 2, :] for d in range(4)
    ]
    put_outgoing([up, down, right, left], (oa, ob, oc, od))


def combine_kernel(own_ref, ra, rb, rc, rd, list_ref, v_ref, small_ref,
                   next_ref, oa, ob, oc, od):
    lists = list_ref[...]
    back = from_swaps([ra, rb, rc, rd])
    terms = jnp.concatenate([b[0:1] for b in back] + [b[1:2] for b in back], axis=0)
    added = scatter_block(lists, terms, OWN_ROWS)
    value = (small_ref[MASS_ROWS, :] * v_ref[0:OWN_ROWS, :] + own_ref[...] + added) * SCALE
    next_ref[...] = value
    put_outgoing(picked_blocks(value, lists), (oa, ob, oc, od))


def prepare_kernel(small_ref, point_ref, tgt_ref, wide_ref, left_ref, right_ref, row_ref):
    def line(rows):
        return jnp.concatenate([small_ref[r:r + 1, :] for r in range(rows.start, rows.stop)], axis=1)

    third = line(COS_ROWS)
    angle = line(ANGLE_ROWS)
    area = line(AREA_ROWS) * inverse_four_pi
    sine = area * jnp.sqrt(1.0 - third * third)
    points = jnp.concatenate([point_ref[...], jnp.zeros((3, PAD_SLOTS - SLOTS), F32)], axis=1)
    src = jnp.concatenate(
        [points, sine * jnp.cos(angle), sine * jnp.sin(angle), area * third, jnp.zeros((2, PAD_SLOTS), F32)],
        axis=0,
    )
    cols = jnp.transpose(src)
    for c in range(6):
        wide_ref[c] = jnp.broadcast_to(cols[0:SLOTS, c:c + 1], (SLOTS, LANES))
    lane = lax.broadcasted_iota(jnp.int32, (TGT_ROWS, LANES), 1)
    for c in range(3):
        out = jnp.zeros((TGT_ROWS, LANES), F32)
        for j in range(4):
            part = tgt_ref[pl.ds(j, TGT_ROWS, stride=4), :]
            shift = (32 * j - 32 * c) % LANES
            if shift:
                part = pltpu.roll(part, shift, 1)
            out = jnp.where((lane >= 32 * j) & (lane < 32 * j + 32), part, out)
        row_ref[c] = out

    def factors(points, scale, extra, swap):
        norm = points[0] * points[0] + points[1] * points[1] + points[2] * points[2] + extra
        ones = jnp.ones_like(norm)
        lines = []
        for p in points:
            a = [q.astype(F32) for q in split_terms(p * scale, 3)]
            order = (0, 1, 0, 1, 2, 0) if swap else (0, 0, 1, 1, 0, 2)
            lines += [a[k] for k in order]
        norms = [q.astype(F32) for q in split_terms(norm, 3)]
        lines += [ones] * 3 + norms if swap else norms + [ones] * 3
        return lines

    left = factors([src[c:c + 1, :] - 0.5 for c in range(3)], 1.0, 0.0, False)
    left = jnp.concatenate(left + [jnp.zeros((KDIM - 24, PAD_SLOTS), F32)], axis=0)
    left_ref[...] = jnp.transpose(left)[0:SLOTS, :].astype(BF16)
    right = factors([row_ref[c] - 0.5 for c in range(3)], -2.0, smoothing, True)
    zero = jnp.zeros((1, LANES), F32)
    for g in range(TGT_ROWS):
        block = jnp.concatenate([r[g:g + 1, :] for r in right] + [zero] * (KDIM - 24), axis=0)
        right_ref[:, g * LANES:(g + 1) * LANES] = block.astype(BF16)


def entries_kernel(base, wide_ref, left_ref, right_ref, row_ref, entry_ref):
    def target_group(g, carry):
        first = base + g * GROUP
        lanes = pl.ds(pl.multiple_of(first * LANES, GROUP * LANES), GROUP * LANES)
        square = jnp.dot(left_ref[...], right_ref[:, lanes], preferred_element_type=F32)
        for s in range(SLOTS // 16):
            rows = slice(16 * s, 16 * s + 16)
            sx, sy, sz, wx, wy, wz = [wide_ref[c, rows, :] for c in range(6)]
            for q in range(GROUP):
                at = pl.ds(first + q, 1)
                inverse = lax.rsqrt(square[rows, q * LANES:(q + 1) * LANES])
                numerator = (
                    (row_ref[0, at, :] - sx) * wx
                    + (row_ref[1, at, :] - sy) * wy
                    + (row_ref[2, at, :] - sz) * wz
                )
                value = (numerator * (inverse * inverse * inverse)).astype(BF16)
                out = pl.ds(pl.multiple_of((g * GROUP + q) * LANES, LANES), LANES)
                entry_ref[rows, out] = value
        return carry

    lax.fori_loop(0, entry_ref.shape[1] // (GROUP * LANES), target_group, 0)


def energy_kernel(live_ref, v2_ref, ga, gb, gc, gd, data_ref, partial_ref, out_ref, ext_ref, turn_ref):
    ext_ref[...] = extend(v2_ref[...], [ga, gb, gc, gd])
    live = live_ref[0]

    def energy_of(t, slot):
        _, _, volume, field = element_gradient(
            ext_ref[...], data_ref, turn_ref.at[slot], jnp.minimum(t, BLOCKS - 1)
        )
        return jnp.where(t < live, volume, 0.0) * (
            field[0] * field[0] + field[1] * field[1] + field[2] * field[2]
        )

    def energy_pair(i, total):
        return total + energy_of(2 * i, 0) + energy_of(2 * i + 1, 1)

    energy = lax.fori_loop(0, (live + 1) // 2, energy_pair, jnp.zeros((8, LANES), F32))
    lane = lax.broadcasted_iota(jnp.int32, (1, LANES), 1)
    share = jnp.where(lane == 101, jnp.sum(energy) * SCALE, 0.0)
    out_ref[...] = partial_ref[...] + share


def far_kernel(small_ref, v1_ref, v2_ref, node_ref, e0, e1, e2,
               out_ref, trace_ref, d0, d1, d2, lhs_ref):
    b = small_ref[B_ROWS, :]
    v1 = v1_ref[...]
    v2 = v2_ref[...]
    products = [b * b, b * v1, v1 * v1, v1 * v2, v2 * v2, small_ref[MASS_ROWS, :] * v2 * v2]
    sums = [p[0:8] + p[8:16] for p in products]
    sums[5] = sums[5] * SCALE
    sub = lax.broadcasted_iota(jnp.int32, (8, LANES), 0)
    lane_row = lax.broadcasted_iota(jnp.int32, (1, LANES), 1)
    moments = jnp.zeros((1, LANES), F32)
    for k in range(6):
        moments = jnp.where(lane_row == 96 + k, jnp.sum(sums[k]), moments)

    nodes = node_ref[...]
    traces = [gather_rows(table, nodes) for table in (b, v1, v2)]
    for k in range(3):
        trace_ref[k] = traces[k]
    for r in range(PAD_SLOTS // LANES):
        block = jnp.zeros((8, LANES), F32)
        for k in range(3):
            t = traces[k][r:r + 1, :]
            high = t.astype(BF16).astype(F32)
            block = jnp.where(sub == 2 * k, high, block)
            block = jnp.where(sub == 2 * k + 1, t - high, block)
        lhs_ref[:, r * LANES:(r + 1) * LANES] = block.astype(BF16)
    lhs = lhs_ref[:, 0:SLOTS]
    base = 0
    for each, entry_ref in zip(CHUNKS, (e0, e1, e2)):
        res = jnp.dot(lhs, entry_ref[...], preferred_element_type=F32)
        base += each
        for q in range(each):
            at = slice(base - each + q, base - each + q + 1)
            part = res[:, q * LANES:(q + 1) * LANES]
            d0[at, :] = part[0:1] + part[1:2]
            d1[at, :] = part[2:3] + part[3:4]
            d2[at, :] = part[4:5] + part[5:6]

    lane = lax.broadcasted_iota(jnp.int32, (TGT_ROWS, LANES), 1)
    spread = jnp.broadcast_to(moments, (TGT_ROWS, LANES))
    for j in range(4):
        out = spread
        for k, ref in enumerate((d0, d1, d2)):
            part = ref[...]
            shift = (32 * k - 32 * j) % LANES
            if shift:
                part = pltpu.roll(part, shift, 1)
            out = jnp.where((lane >= 32 * k) & (lane < 32 * k + 32), part, out)
        out_ref[pl.ds(j, TGT_ROWS, stride=4), :] = out


def final_kernel(got_ref, small_ref, v1_ref, v2_ref, trace_ref, pot_ref, dir_ref):
    total = jnp.sum(got_ref[...], axis=0, keepdims=True)
    lane = lax.broadcasted_iota(jnp.int32, (1, LANES), 1)
    m = [jnp.sum(jnp.where(lane == 96 + k, total, 0.0), axis=1, keepdims=True) for k in range(6)]
    l1 = m[2] / m[1]
    l2 = m[3] / m[1]
    s11 = m[3] - l1 * m[2]
    s12 = m[4] - l1 * m[3]
    s22 = m[5] - l2 * m[3]
    y1 = m[1] - l1 * m[0]
    y2 = m[2] - l2 * m[0]
    keep1 = s11 > 4e-7 * m[3]
    safe11 = jnp.where(keep1, s11, 1.0)
    ratio = jnp.where(keep1, s12 / safe11, 0.0)
    d2 = s22 - ratio * s12
    keep2 = keep1 & (d2 > 4e-7 * m[5])
    c2 = jnp.where(keep2, (y2 - ratio * y1) / jnp.where(keep2, d2, 1.0), 0.0)
    c1 = jnp.where(keep1, (y1 - s12 * c2) / safe11, 0.0)
    c0 = (m[0] - m[2] * c1 - m[3] * c2) / m[1]
    c0 = c0 * SCALE
    c1 = c1 * SCALE
    c2 = c2 * SCALE
    pot_ref[...] = c0 * small_ref[B_ROWS, :] + c1 * v1_ref[...] + c2 * v2_ref[...]
    out = jnp.zeros((1, LANES), F32)
    for k, c in enumerate((c0, c1, c2)):
        part = total
        if k:
            part = pltpu.roll(total, LANES - 32 * k, 1)
        out = out + c * (part - 0.5 * trace_ref[k, 0:1, :])
    dir_ref[...] = out[:, 0:TGT_DEV]


def call(body, out_shapes, args, smem=0, scratch=(), cost=2000000):
    specs = [pl.BlockSpec(memory_space=pltpu.SMEM)] * smem
    specs += [pl.BlockSpec(memory_space=pltpu.VMEM)] * (len(args) - smem)
    out_shapes = [o if isinstance(o, jax.ShapeDtypeStruct) else jax.ShapeDtypeStruct(o, F32) for o in out_shapes]
    return pl.pallas_call(
        body,
        out_shape=out_shapes,
        in_specs=specs,
        out_specs=[pl.BlockSpec(memory_space=pltpu.VMEM)] * len(out_shapes),
        scratch_shapes=list(scratch),
        compiler_params=pltpu.CompilerParams(vmem_limit_bytes=VMEM_GRANT),
        cost_estimate=pl.CostEstimate(flops=cost, bytes_accessed=1 << 20, transcendentals=0),
    )(*args)


PIECE = (2, LANES)
TURN = pltpu.VMEM((128, LANES), F32)


def swap_partners(rows, cols, axis, second):
    out = []
    for r in range(rows):
        for c in range(cols):
            me, count = (r, rows) if axis == "row" else (c, cols)
            if not second:
                other = me ^ 1
            elif 0 < me < count - 1:
                other = ((me + 1) ^ 1) - 1
            else:
                other = None
            if axis == "row":
                pair = (other, c) if other is not None else (r, c ^ 1)
            else:
                pair = (r, other) if other is not None else (r ^ 1, c)
            out.append((r * cols + c, pair[0] * cols + pair[1]))
    return out


def exchange(pieces):
    rows = lax.axis_size("row")
    cols = lax.axis_size("col")
    got = []
    for k in range(4):
        axis = "row" if k < 2 else "col"
        got.append(lax.ppermute(pieces[k], ("row", "col"), swap_partners(rows, cols, axis, k % 2 == 1)))
    return got


def per_device(connectivity, gradients, volumes, live_blocks, send_lists, divergence, mass_shift,
               boundary_nodes, surface_points, normal_cos, normal_angle, node_areas):
    lists = send_lists.reshape(4, 2, LANES).transpose(1, 0, 2).reshape(8, LANES)
    nodes = jnp.pad(boundary_nodes, (0, 8 * LANES - SLOTS)).reshape(8, LANES)
    gap = jnp.zeros(PAD_SLOTS - SLOTS, F32)
    small = jnp.concatenate([
        divergence, mass_shift, normal_cos, gap, normal_angle, gap, node_areas, gap,
    ]).reshape(-1, LANES)
    data = jnp.concatenate([gradients, connectivity.astype(F32), volumes[None]], axis=0)
    mine, lists, points, *pieces = call(
        pick_kernel,
        [(N_DEV, LANES), jax.ShapeDtypeStruct(lists.shape, lists.dtype), surface_points.shape] + [PIECE] * 4,
        (small, lists, surface_points),
    )
    targets = lax.all_to_all(mine, ("row", "col"), 0, 0, tiled=True)
    prepared = None
    chunks = []

    def fill():
        nonlocal prepared
        if prepared is None:
            prepared = call(
                prepare_kernel,
                [
                    (6, SLOTS, LANES),
                    jax.ShapeDtypeStruct((SLOTS, KDIM), BF16),
                    jax.ShapeDtypeStruct((KDIM, TGT_ROWS * LANES), BF16),
                    (3, TGT_ROWS, LANES),
                ],
                (small, points, targets),
            )
            return
        done = len(chunks)
        base = sum(CHUNKS[:done])
        chunks.append(call(
            lambda *refs: entries_kernel(base, *refs),
            [jax.ShapeDtypeStruct((SLOTS, CHUNKS[done] * LANES), BF16)],
            prepared,
        )[0])

    def swap(number, pieces):
        out = exchange(pieces)
        if number:
            fill()
        return out

    vectors = [small]
    for step in range(2):
        ghosts = swap(2 * step, pieces)
        own, *back = call(
            apply_kernel, [(OWN_ROWS, LANES)] + [PIECE] * 4,
            (live_blocks, vectors[-1], *ghosts, data), smem=1,
            scratch=[pltpu.VMEM((EXT_ROWS, LANES), F32), pltpu.VMEM((HIGH_ROWS, LANES), F32), TURN],
        )
        returned = swap(2 * step + 1, back)
        new, *pieces = call(
            combine_kernel, [(OWN_ROWS, LANES)] + [PIECE] * 4,
            (own, *returned, lists, vectors[-1], small),
        )
        vectors.append(new)
    ghosts = exchange(pieces)
    fill()
    partial, trace = call(
        far_kernel, [(N_DEV, LANES), (3, 8, LANES)], (*vectors, nodes, *chunks),
        scratch=[pltpu.VMEM((TGT_ROWS, LANES), F32)] * 3 + [pltpu.VMEM((8, PAD_SLOTS), BF16)],
    )
    partial, = call(
        energy_kernel, [(N_DEV, LANES)], (live_blocks, vectors[-1], *ghosts, data, partial), smem=1,
        scratch=[pltpu.VMEM((EXT_ROWS, LANES), F32), pltpu.VMEM((2, 128, LANES), F32)],
    )
    got = lax.all_to_all(partial, ("row", "col"), 0, 0, tiled=True)
    potential, dirichlet = call(
        final_kernel, [(OWN_ROWS, LANES), (1, TGT_DEV)], (got, *vectors, trace)
    )
    return potential.reshape(NN_DEV), dirichlet.reshape(TGT_DEV)


def solution(mesh):
    both = ("row", "col")

    return jax.shard_map(
        per_device,
        mesh=mesh,
        in_specs=(
            P(None, both), P(None, both), P(both), P(both), P(None, both), P(both),
            P(both), P(both), P(None, both), P(both), P(both), P(both),
        ),
        out_specs=(P(both), P(both)),
        check_vma=False,
    )
```

```python
import math

import jax
import jax.numpy as jnp
from jax import lax
from jax.experimental import pallas as pl
from jax.experimental.pallas import tpu as pltpu
from jax.sharding import PartitionSpec as P


F32 = jnp.float32
BF16 = jnp.bfloat16
LANES = 128
NN_DEV = 2048
EBLK = 1024
BLOCKS = 8
GH = 256
TGT_DEV = 32
OWN_ROWS = NN_DEV // LANES
EXT_ROWS = OWN_ROWS + 4 * GH // LANES
HIGH_ROWS = 32
ELEM_ROWS = 64
SLOTS = 320
PAD_SLOTS = 384
N_DEV = 256
TGT_ROWS = N_DEV // 4
CHUNKS = (16, 16, 20, 12)
GROUP = 4
KDIM = 32
SPLITS = 2
SCALE = 1.0 / 64.0
B_ROWS = slice(0, 16)
MASS_ROWS = slice(16, 32)
COS_ROWS = slice(32, 35)
ANGLE_ROWS = slice(35, 38)
AREA_ROWS = slice(38, 41)
VMEM_GRANT = 16 << 20
smoothing = 0.0001
inverse_four_pi = 1.0 / (4.0 * math.pi)


def gather_rows(table, index):
    high = index >> 7
    low = index & 127
    out = jnp.zeros(index.shape, F32)
    for r in range(table.shape[0]):
        row = jnp.broadcast_to(table[r:r + 1, :], index.shape)
        out = jnp.where(high == r, jnp.take_along_axis(row, low, axis=1), out)
    return out


def split_terms(terms, count):
    parts = []
    for _ in range(count):
        parts.append(terms.astype(BF16))
        terms = terms - parts[-1].astype(F32)
    return parts


def scatter_block(index, terms, rows):
    rows = -(-rows // 16) * 16
    sub = lax.broadcasted_iota(jnp.int32, (LANES, LANES), 0).astype(F32).astype(BF16)
    sub_rows = lax.broadcasted_iota(jnp.int32, (rows, LANES), 0).astype(F32).astype(BF16)
    one = jnp.ones((LANES, LANES), BF16)
    zero = jnp.zeros((LANES, LANES), BF16)
    zero_rows = jnp.zeros((rows, LANES), BF16)
    low = (index & 127).astype(F32)
    high = (index >> 7).astype(F32)
    parts = [p.astype(F32) for p in split_terms(terms, SPLITS)]
    hot_blocks = []
    weight_blocks = []
    for s in range(8):
        at = slice(s, s + 1)
        low_row = jnp.broadcast_to(low[at], (LANES, LANES)).astype(BF16)
        hot_blocks.append(jnp.where(sub == low_row, one, zero))
        mine = sub_rows == jnp.broadcast_to(high[at], (rows, LANES)).astype(BF16)
        weight_blocks.append(jnp.concatenate(
            [jnp.where(mine, jnp.broadcast_to(p[at], (rows, LANES)).astype(BF16), zero_rows) for p in parts],
            axis=0,
        ))
    total = lax.dot_general(
        jnp.concatenate(weight_blocks, axis=1), jnp.concatenate(hot_blocks, axis=1),
        (((1,), (1,)), ((), ())), preferred_element_type=F32,
    )
    out = total[0:rows]
    for k in range(1, SPLITS):
        out = out + total[k * rows:(k + 1) * rows]
    return out


def turn_block(data_ref, turn_ref, t):
    for k in range(8):
        lanes = pl.ds(pl.multiple_of(EBLK * t + LANES * k, LANES), LANES)
        turn_ref[16 * k:16 * k + 8, :] = data_ref[0:8, lanes]
        turn_ref[16 * k + 8:16 * k + 10, :] = data_ref[8:10, lanes]
    rows = [turn_ref[pl.ds(q, 8, stride=16), :] for q in range(10)]
    return rows[0:9], rows[9]


def element_gradient(ext, data_ref, conn_ref, turn_ref, t):
    grads, volume = turn_block(data_ref, turn_ref, t)
    index = [conn_ref[pl.ds(32 * t + a, 8, stride=4), :] for a in range(4)]
    corner = [gather_rows(ext, i) for i in index]
    diff = [corner[a] - corner[3] for a in range(3)]
    field = [
        grads[k] * diff[0] + grads[3 + k] * diff[1] + grads[6 + k] * diff[2]
        for k in range(3)
    ]
    return grads, index, volume, field


def odd(axis):
    return lax.rem(lax.axis_index(axis), 2) == 1


def inside(axis):
    me = lax.axis_index(axis)
    return (me > 0) & (me < lax.axis_size(axis) - 1)


def from_swaps(pieces):
    row_a, row_b, col_a, col_b = [p[...] for p in pieces]
    row_b = jnp.where(inside("row"), row_b, 0.0)
    col_b = jnp.where(inside("col"), col_b, 0.0)
    row_odd = odd("row")
    col_odd = odd("col")
    return [
        jnp.where(row_odd, row_b, row_a),
        jnp.where(row_odd, row_a, row_b),
        jnp.where(col_odd, col_b, col_a),
        jnp.where(col_odd, col_a, col_b),
    ]


def put_outgoing(blocks, out_refs):
    row_odd = odd("row")
    col_odd = odd("col")
    out_refs[0][...] = jnp.where(row_odd, blocks[1], blocks[0])
    out_refs[1][...] = jnp.where(row_odd, blocks[0], blocks[1])
    out_refs[2][...] = jnp.where(col_odd, blocks[3], blocks[2])
    out_refs[3][...] = jnp.where(col_odd, blocks[2], blocks[3])


def extend(v, pieces):
    up, down, right, left = from_swaps(pieces)
    return jnp.concatenate([v, down, up, left, right], axis=0)


def picked_blocks(v, lists):
    got = gather_rows(v, lists)
    return [jnp.concatenate([got[d:d + 1], got[4 + d:5 + d]], axis=0) for d in range(4)]


def pick_kernel(small_ref, list_ref, point_ref, target_ref, same_list_ref, same_point_ref, *out_refs):
    same_list_ref[...] = list_ref[...]
    same_point_ref[...] = point_ref[...]
    put_outgoing(picked_blocks(small_ref[B_ROWS, :], list_ref[...]), out_refs)
    lane = lax.broadcasted_iota(jnp.int32, (1, LANES), 1)
    own = jnp.zeros((1, LANES), F32)
    for c in range(3):
        part = point_ref[c:c + 1, 0:LANES]
        if c:
            part = pltpu.roll(part, TGT_DEV * c, 1)
        own = jnp.where((lane >= TGT_DEV * c) & (lane < TGT_DEV * (c + 1)), part, own)
    target_ref[...] = jnp.broadcast_to(own, (N_DEV, LANES))


def apply_kernel(live_ref, v_ref, ga, gb, gc, gd, data_ref, conn_ref,
                 own_ref, oa, ob, oc, od, ext_ref, acc_ref, turn_ref):
    ext_ref[...] = extend(v_ref[0:OWN_ROWS, :], [ga, gb, gc, gd])
    acc_ref[...] = jnp.zeros_like(acc_ref)

    def element_terms(t):
        grads, index, volume, field = element_gradient(
            ext_ref[...], data_ref, conn_ref, turn_ref, jnp.minimum(t, BLOCKS - 1)
        )
        field = [volume * f for f in field]
        terms = [
            grads[3 * a] * field[0] + grads[3 * a + 1] * field[1] + grads[3 * a + 2] * field[2]
            for a in range(3)
        ]
        terms.append(-(terms[0] + terms[1] + terms[2]))
        return tuple(index), tuple(terms)

    def element_block(t, carry):
        index, terms = carry
        following = element_terms(t + 1)
        total = acc_ref[...]
        for a in range(4):
            total = total + scatter_block(index[a], terms[a], EXT_ROWS)
        acc_ref[...] = total
        return following

    lax.fori_loop(0, live_ref[0], element_block, element_terms(0))
    own_ref[...] = acc_ref[0:OWN_ROWS, :]
    down, up, left, right = [
        acc_ref[OWN_ROWS + 2 * d:OWN_ROWS + 2 * d + 2, :] for d in range(4)
    ]
    put_outgoing([up, down, right, left], (oa, ob, oc, od))


def combine_kernel(own_ref, ra, rb, rc, rd, list_ref, v_ref, small_ref,
                   next_ref, oa, ob, oc, od):
    lists = list_ref[...]
    back = from_swaps([ra, rb, rc, rd])
    terms = jnp.concatenate([b[0:1] for b in back] + [b[1:2] for b in back], axis=0)
    added = scatter_block(lists, terms, OWN_ROWS)
    value = (small_ref[MASS_ROWS, :] * v_ref[0:OWN_ROWS, :] + own_ref[...] + added) * SCALE
    next_ref[...] = value
    put_outgoing(picked_blocks(value, lists), (oa, ob, oc, od))


def prepare_kernel(small_ref, point_ref, tgt_ref, wide_ref, left_ref, right_ref, row_ref):
    def line(rows):
        return jnp.concatenate([small_ref[r:r + 1, :] for r in range(rows.start, rows.stop)], axis=1)

    third = line(COS_ROWS)
    angle = line(ANGLE_ROWS)
    area = line(AREA_ROWS) * inverse_four_pi
    sine = area * jnp.sqrt(1.0 - third * third)
    points = jnp.concatenate([point_ref[...], jnp.zeros((3, PAD_SLOTS - SLOTS), F32)], axis=1)
    src = jnp.concatenate(
        [points, sine * jnp.cos(angle), sine * jnp.sin(angle), area * third, jnp.zeros((2, PAD_SLOTS), F32)],
        axis=0,
    )
    cols = jnp.transpose(src)
    for c in range(6):
        wide_ref[c] = jnp.broadcast_to(cols[0:SLOTS, c:c + 1], (SLOTS, LANES))
    lane = lax.broadcasted_iota(jnp.int32, (TGT_ROWS, LANES), 1)
    for c in range(3):
        out = jnp.zeros((TGT_ROWS, LANES), F32)
        for j in range(4):
            part = tgt_ref[pl.ds(j, TGT_ROWS, stride=4), :]
            shift = (32 * j - 32 * c) % LANES
            if shift:
                part = pltpu.roll(part, shift, 1)
            out = jnp.where((lane >= 32 * j) & (lane < 32 * j + 32), part, out)
        row_ref[c] = out

    def factors(points, scale, extra, swap):
        norm = points[0] * points[0] + points[1] * points[1] + points[2] * points[2] + extra
        ones = jnp.ones_like(norm)
        lines = []
        for p in points:
            a = [q.astype(F32) for q in split_terms(p * scale, 3)]
            order = (0, 1, 0, 1, 2, 0) if swap else (0, 0, 1, 1, 0, 2)
            lines += [a[k] for k in order]
        norms = [q.astype(F32) for q in split_terms(norm, 3)]
        lines += [ones] * 3 + norms if swap else norms + [ones] * 3
        return lines

    left = factors([src[c:c + 1, :] - 0.5 for c in range(3)], 1.0, 0.0, False)
    left = jnp.concatenate(left + [jnp.zeros((KDIM - 24, PAD_SLOTS), F32)], axis=0)
    left_ref[...] = jnp.transpose(left)[0:SLOTS, :].astype(BF16)
    right = factors([row_ref[c] - 0.5 for c in range(3)], -2.0, smoothing, True)
    zero = jnp.zeros((1, LANES), F32)
    for g in range(TGT_ROWS):
        block = jnp.concatenate([r[g:g + 1, :] for r in right] + [zero] * (KDIM - 24), axis=0)
        right_ref[:, g * LANES:(g + 1) * LANES] = block.astype(BF16)


def entries_kernel(base, wide_ref, left_ref, right_ref, row_ref, entry_ref):
    def target_group(g, carry):
        first = base + g * GROUP
        lanes = pl.ds(pl.multiple_of(first * LANES, GROUP * LANES), GROUP * LANES)
        square = jnp.dot(left_ref[...], right_ref[:, lanes], preferred_element_type=F32)
        for s in range(SLOTS // 16):
            rows = slice(16 * s, 16 * s + 16)
            sx, sy, sz, wx, wy, wz = [wide_ref[c, rows, :] for c in range(6)]
            for q in range(GROUP):
                at = pl.ds(first + q, 1)
                inverse = lax.rsqrt(square[rows, q * LANES:(q + 1) * LANES])
                numerator = (
                    (row_ref[0, at, :] - sx) * wx
                    + (row_ref[1, at, :] - sy) * wy
                    + (row_ref[2, at, :] - sz) * wz
                )
                value = (numerator * (inverse * inverse * inverse)).astype(BF16)
                out = pl.ds(pl.multiple_of((g * GROUP + q) * LANES, LANES), LANES)
                entry_ref[rows, out] = value
        return carry

    lax.fori_loop(0, entry_ref.shape[1] // (GROUP * LANES), target_group, 0)


def energy_kernel(live_ref, v2_ref, ga, gb, gc, gd, data_ref, conn_ref, partial_ref,
                  out_ref, ext_ref, turn_ref):
    ext_ref[...] = extend(v2_ref[...], [ga, gb, gc, gd])
    live = live_ref[0]

    def energy_of(t, slot):
        _, _, volume, field = element_gradient(
            ext_ref[...], data_ref, conn_ref, turn_ref.at[slot], jnp.minimum(t, BLOCKS - 1)
        )
        return jnp.where(t < live, volume, 0.0) * (
            field[0] * field[0] + field[1] * field[1] + field[2] * field[2]
        )

    def energy_pair(i, total):
        return total + energy_of(2 * i, 0) + energy_of(2 * i + 1, 1)

    energy = lax.fori_loop(0, (live + 1) // 2, energy_pair, jnp.zeros((8, LANES), F32))
    lane = lax.broadcasted_iota(jnp.int32, (1, LANES), 1)
    share = jnp.where(lane == 101, jnp.sum(energy) * SCALE, 0.0)
    out_ref[...] = partial_ref[...] + share


def far_kernel(small_ref, v1_ref, v2_ref, node_ref, e0, e1, e2, e3,
               out_ref, trace_ref, d0, d1, d2, lhs_ref):
    b = small_ref[B_ROWS, :]
    v1 = v1_ref[...]
    v2 = v2_ref[...]
    products = [b * b, b * v1, v1 * v1, v1 * v2, v2 * v2, small_ref[MASS_ROWS, :] * v2 * v2]
    sums = [p[0:8] + p[8:16] for p in products]
    sums[5] = sums[5] * SCALE
    sub = lax.broadcasted_iota(jnp.int32, (8, LANES), 0)
    lane_row = lax.broadcasted_iota(jnp.int32, (1, LANES), 1)
    moments = jnp.zeros((1, LANES), F32)
    for k in range(6):
        moments = jnp.where(lane_row == 96 + k, jnp.sum(sums[k]), moments)

    nodes = node_ref[...]
    traces = [gather_rows(table, nodes) for table in (b, v1, v2)]
    for k in range(3):
        trace_ref[k] = traces[k]
    for r in range(PAD_SLOTS // LANES):
        block = jnp.zeros((8, LANES), F32)
        for k in range(3):
            t = traces[k][r:r + 1, :]
            high = t.astype(BF16).astype(F32)
            block = jnp.where(sub == 2 * k, high, block)
            block = jnp.where(sub == 2 * k + 1, t - high, block)
        lhs_ref[:, r * LANES:(r + 1) * LANES] = block.astype(BF16)
    lhs = lhs_ref[:, 0:SLOTS]
    base = 0
    for each, entry_ref in zip(CHUNKS, (e0, e1, e2, e3)):
        res = jnp.dot(lhs, entry_ref[...], preferred_element_type=F32)
        base += each
        for q in range(each):
            at = slice(base - each + q, base - each + q + 1)
            part = res[:, q * LANES:(q + 1) * LANES]
            d0[at, :] = part[0:1] + part[1:2]
            d1[at, :] = part[2:3] + part[3:4]
            d2[at, :] = part[4:5] + part[5:6]

    lane = lax.broadcasted_iota(jnp.int32, (TGT_ROWS, LANES), 1)
    spread = jnp.broadcast_to(moments, (TGT_ROWS, LANES))
    for j in range(4):
        out = spread
        for k, ref in enumerate((d0, d1, d2)):
            part = ref[...]
            shift = (32 * k - 32 * j) % LANES
            if shift:
                part = pltpu.roll(part, shift, 1)
            out = jnp.where((lane >= 32 * k) & (lane < 32 * k + 32), part, out)
        out_ref[pl.ds(j, TGT_ROWS, stride=4), :] = out


def final_kernel(got_ref, small_ref, v1_ref, v2_ref, trace_ref, pot_ref, dir_ref):
    total = jnp.sum(got_ref[...], axis=0, keepdims=True)
    lane = lax.broadcasted_iota(jnp.int32, (1, LANES), 1)
    m = [jnp.sum(jnp.where(lane == 96 + k, total, 0.0), axis=1, keepdims=True) for k in range(6)]
    l1 = m[2] / m[1]
    l2 = m[3] / m[1]
    s11 = m[3] - l1 * m[2]
    s12 = m[4] - l1 * m[3]
    s22 = m[5] - l2 * m[3]
    y1 = m[1] - l1 * m[0]
    y2 = m[2] - l2 * m[0]
    keep1 = s11 > 4e-7 * m[3]
    safe11 = jnp.where(keep1, s11, 1.0)
    ratio = jnp.where(keep1, s12 / safe11, 0.0)
    d2 = s22 - ratio * s12
    keep2 = keep1 & (d2 > 4e-7 * m[5])
    c2 = jnp.where(keep2, (y2 - ratio * y1) / jnp.where(keep2, d2, 1.0), 0.0)
    c1 = jnp.where(keep1, (y1 - s12 * c2) / safe11, 0.0)
    c0 = (m[0] - m[2] * c1 - m[3] * c2) / m[1]
    c0 = c0 * SCALE
    c1 = c1 * SCALE
    c2 = c2 * SCALE
    pot_ref[...] = c0 * small_ref[B_ROWS, :] + c1 * v1_ref[...] + c2 * v2_ref[...]
    out = jnp.zeros((1, LANES), F32)
    for k, c in enumerate((c0, c1, c2)):
        part = total
        if k:
            part = pltpu.roll(total, LANES - 32 * k, 1)
        out = out + c * (part - 0.5 * trace_ref[k, 0:1, :])
    dir_ref[...] = out[:, 0:TGT_DEV]


def call(body, out_shapes, args, smem=0, scratch=(), cost=2000000):
    specs = [pl.BlockSpec(memory_space=pltpu.SMEM)] * smem
    specs += [pl.BlockSpec(memory_space=pltpu.VMEM)] * (len(args) - smem)
    out_shapes = [o if isinstance(o, jax.ShapeDtypeStruct) else jax.ShapeDtypeStruct(o, F32) for o in out_shapes]
    return pl.pallas_call(
        body,
        out_shape=out_shapes,
        in_specs=specs,
        out_specs=[pl.BlockSpec(memory_space=pltpu.VMEM)] * len(out_shapes),
        scratch_shapes=list(scratch),
        compiler_params=pltpu.CompilerParams(vmem_limit_bytes=VMEM_GRANT),
        cost_estimate=pl.CostEstimate(flops=cost, bytes_accessed=1 << 20, transcendentals=0),
    )(*args)


PIECE = (2, LANES)
TURN = pltpu.VMEM((128, LANES), F32)


def swap_partners(rows, cols, axis, second):
    out = []
    for r in range(rows):
        for c in range(cols):
            me, count = (r, rows) if axis == "row" else (c, cols)
            if not second:
                other = me ^ 1
            elif 0 < me < count - 1:
                other = ((me + 1) ^ 1) - 1
            else:
                other = None
            if axis == "row":
                pair = (other, c) if other is not None else (r, c ^ 1)
            else:
                pair = (r, other) if other is not None else (r ^ 1, c)
            out.append((r * cols + c, pair[0] * cols + pair[1]))
    return out


def exchange(pieces):
    rows = lax.axis_size("row")
    cols = lax.axis_size("col")
    got = []
    for k in range(4):
        axis = "row" if k < 2 else "col"
        got.append(lax.ppermute(pieces[k], ("row", "col"), swap_partners(rows, cols, axis, k % 2 == 1)))
    return got


def per_device(connectivity, gradients, volumes, live_blocks, send_lists, divergence, mass_shift,
               boundary_nodes, surface_points, normal_cos, normal_angle, node_areas):
    lists = send_lists.reshape(4, 2, LANES).transpose(1, 0, 2).reshape(8, LANES)
    nodes = jnp.pad(boundary_nodes, (0, 8 * LANES - SLOTS)).reshape(8, LANES)
    gap = jnp.zeros(PAD_SLOTS - SLOTS, F32)
    small = jnp.concatenate([
        divergence, mass_shift, normal_cos, gap, normal_angle, gap, node_areas, gap,
    ]).reshape(-1, LANES)
    data = jnp.concatenate([gradients, volumes[None]], axis=0)
    conn = connectivity.reshape(4, ELEM_ROWS, LANES).transpose(1, 0, 2).reshape(4 * ELEM_ROWS, LANES)
    mine, lists, points, *pieces = call(
        pick_kernel,
        [(N_DEV, LANES), jax.ShapeDtypeStruct(lists.shape, lists.dtype), surface_points.shape] + [PIECE] * 4,
        (small, lists, surface_points),
    )
    targets = lax.all_to_all(mine, ("row", "col"), 0, 0, tiled=True)
    prepared = None
    chunks = []

    def fill():
        nonlocal prepared
        if prepared is None:
            prepared = call(
                prepare_kernel,
                [
                    (6, SLOTS, LANES),
                    jax.ShapeDtypeStruct((SLOTS, KDIM), BF16),
                    jax.ShapeDtypeStruct((KDIM, TGT_ROWS * LANES), BF16),
                    (3, TGT_ROWS, LANES),
                ],
                (small, points, targets),
            )
        done = len(chunks)
        base = sum(CHUNKS[:done])
        chunks.append(call(
            lambda *refs: entries_kernel(base, *refs),
            [jax.ShapeDtypeStruct((SLOTS, CHUNKS[done] * LANES), BF16)],
            prepared,
        )[0])

    def swap(number, pieces):
        out = exchange(pieces)
        if number:
            fill()
        return out

    vectors = [small]
    for step in range(2):
        ghosts = swap(2 * step, pieces)
        own, *back = call(
            apply_kernel, [(OWN_ROWS, LANES)] + [PIECE] * 4,
            (live_blocks, vectors[-1], *ghosts, data, conn), smem=1,
            scratch=[pltpu.VMEM((EXT_ROWS, LANES), F32), pltpu.VMEM((HIGH_ROWS, LANES), F32), TURN],
        )
        returned = swap(2 * step + 1, back)
        new, *pieces = call(
            combine_kernel, [(OWN_ROWS, LANES)] + [PIECE] * 4,
            (own, *returned, lists, vectors[-1], small),
        )
        vectors.append(new)
    ghosts = exchange(pieces)
    fill()
    partial, trace = call(
        far_kernel, [(N_DEV, LANES), (3, 8, LANES)], (*vectors, nodes, *chunks),
        scratch=[pltpu.VMEM((TGT_ROWS, LANES), F32)] * 3 + [pltpu.VMEM((8, PAD_SLOTS), BF16)],
    )
    partial, = call(
        energy_kernel, [(N_DEV, LANES)], (live_blocks, vectors[-1], *ghosts, data, conn, partial), smem=1,
        scratch=[pltpu.VMEM((EXT_ROWS, LANES), F32), pltpu.VMEM((2, 128, LANES), F32)],
    )
    got = lax.all_to_all(partial, ("row", "col"), 0, 0, tiled=True)
    potential, dirichlet = call(
        final_kernel, [(OWN_ROWS, LANES), (1, TGT_DEV)], (got, *vectors, trace)
    )
    return potential.reshape(NN_DEV), dirichlet.reshape(TGT_DEV)


def solution(mesh):
    both = ("row", "col")

    return jax.shard_map(
        per_device,
        mesh=mesh,
        in_specs=(
            P(None, both), P(None, both), P(both), P(both), P(None, both), P(both),
            P(both), P(both), P(None, both), P(both), P(both), P(both),
        ),
        out_specs=(P(both), P(both)),
        check_vma=False,
    )
```
